32 devices in a mesh: blk: 4 (over x, core), grp: 8 (over z, y).
Axes of the slice: x: 2, y: 2, z: 4, core: 2. Of those that a mesh axis runs over, the one named last changes fastest.
Arguments:
- picture_vectors: bfloat16 [12288, 1152], P(('blk', 'grp')), may hold values from -2.3570226 to 2.3570226
- text_vectors: bfloat16 [12288, 1152], P(('blk', 'grp')), may hold values from -2.3570226 to 2.3570226
- matching_text_position: int32 [32, 384], P(('blk', 'grp')), may hold values from 0 to 383, each once within a row
- natural_scale_exponent: float32 [1], replicated, may hold values from 1.5 to 2.3
- offset_added_before_sigmoid: float32 [1], replicated, may hold values from -3 to -1
Outputs:
- image_grad: bfloat16 [12288, 1152], P(('blk', 'grp'))
- caption_grad: bfloat16 [12288, 1152], P(('blk', 'grp'))
The draws below stay inside these ranges and needn't reach their ends.
Inputs may be any that keep to these rules, and one draw needn't show every extreme that they name: `matching_text_position`: each row of positives names every position 0 .. 383 exactly once.
All inputs are finite; a program needn't handle non-finite values.
Results may differ from the reference program's by a relative error of at most 0.0059.
Values may be sent and summed in bfloat16 or wider, within the bound.
A program may use at most 64 MiB of HBM per device.

```python
import math
import jax
import jax.numpy as jnp
from jax import lax

D = 1152
PAIRS = 384
STEPS = 4
BLOCKS = 32
ROWS = 12288


def embedding_draw(key):
    key_rows, key_cols, key_base = jax.random.split(key, 3)
    row_scale = jnp.exp(jax.random.uniform(key_rows, (ROWS, 1), jnp.float32, 0.0, math.log(10.0)))
    col_scale = jnp.exp(jax.random.uniform(key_cols, (1, D), jnp.float32, 0.0, math.log(10.0)))
    base_draw = jax.random.normal(key_base, (ROWS, D), jnp.float32)
    base_draw = jnp.clip(base_draw, -4.0, 4.0)
    values = base_draw * row_scale * col_scale * (0.2 / math.sqrt(D))
    return values.astype(jnp.bfloat16)


def draw_picture_vectors(key, part):
    return embedding_draw(jax.random.fold_in(key, 11))


def draw_text_vectors(key, part):
    return embedding_draw(jax.random.fold_in(key, 23))


def setup_inputs(seed: int = 0) -> dict:
    key_of = jax.random.split(jax.random.key(seed), 6)
    return {
        "picture_vectors": draw_picture_vectors(jax.random.fold_in(key_of[5], 71), 0),
        "text_vectors": draw_text_vectors(jax.random.fold_in(key_of[5], 71), 0),
        "matching_text_position": jax.vmap(lambda own: jax.random.permutation(own, PAIRS))(jax.random.split(key_of[2], BLOCKS)).reshape((BLOCKS, PAIRS)).astype(jnp.int32),
        "natural_scale_exponent": jnp.clip(jax.random.uniform(key_of[3], (1,), jnp.float32, 1.5, 2.3), 1.5, 2.3),
        "offset_added_before_sigmoid": jnp.clip(jax.random.uniform(key_of[4], (1,), jnp.float32, -3.0, -1.0), -3.0, -1.0),
    }


def unit_rows(raw_rows):
    values = raw_rows.astype(jnp.float32)
    inverse_norm = lax.rsqrt(lax.optimization_barrier(jnp.sum(values * values, axis=1, keepdims=True)) + 1e-06)
    return (values * inverse_norm, inverse_norm)

def unit_block(raw_rows):
    return unit_rows(raw_rows)[0].astype(jnp.bfloat16)

def cross_dot_products(picture_entry_slab, window_width_along_diagonal, exponentiated_scale, rotation_offset):
    cosine_table = lax.dot_general(picture_entry_slab, window_width_along_diagonal, (((1,), (1,)), ((), ())), preferred_element_type=jnp.float32)
    return exponentiated_scale * cosine_table + rotation_offset

def sigmoid_cost_coefficients(agreement_table, label_polarity, exponentiated_scale):
    derivative_wrt_presigmoid = -label_polarity * jax.nn.sigmoid(-label_polarity * agreement_table)
    return (exponentiated_scale * derivative_wrt_presigmoid).astype(jnp.bfloat16)

def finish(unit_flat, inverse_norm, direction):
    cosine_table = lax.optimization_barrier(jnp.sum(unit_flat * direction, axis=1, keepdims=True))
    return (inverse_norm * (direction - unit_flat * cosine_table)).astype(jnp.bfloat16)

def reference(picture_vectors, text_vectors, matching_text_position, natural_scale_exponent, offset_added_before_sigmoid):
    exponentiated_scale = jnp.exp(natural_scale_exponent[0])
    rotation_offset = offset_added_before_sigmoid[0]
    midpoint_entries = PAIRS // 2
    image_blocks = picture_vectors.reshape(BLOCKS, PAIRS, D)
    caption_blocks = text_vectors.reshape(BLOCKS, PAIRS, D)
    image_units = lax.map(unit_block, image_blocks)
    caption_units = lax.map(unit_block, caption_blocks)
    columns = lax.broadcasted_iota(jnp.int32, (PAIRS, PAIRS), 1)

    def image_block(block_index):
        device_picture_vectors = image_units[block_index]
        first_labels = jnp.where(columns == matching_text_position[block_index][:, None], 1.0, -1.0).astype(jnp.float32)
        running = jnp.zeros((PAIRS, D), jnp.float32)
        for rotation in range(STEPS):
            upper_half = caption_units[(block_index - rotation) % BLOCKS][:midpoint_entries]
            lower_half = caption_units[(block_index + rotation) % BLOCKS][midpoint_entries:]
            window_width_along_diagonal = jnp.concatenate([upper_half, lower_half], axis=0)
            label_polarity = first_labels if rotation == 0 else -1.0
            coupling_coefficient = sigmoid_cost_coefficients(cross_dot_products(device_picture_vectors, window_width_along_diagonal, exponentiated_scale, rotation_offset), label_polarity, exponentiated_scale)
            running = running + jnp.dot(coupling_coefficient, window_width_along_diagonal, preferred_element_type=jnp.float32)
        unit_flat, inverse_norm = unit_rows(image_blocks[block_index])
        return finish(unit_flat, inverse_norm, running)

    def caption_block(block_index):
        device_text_vectors = caption_units[block_index]
        first_labels = jnp.where(columns == matching_text_position[block_index][:, None], 1.0, -1.0).astype(jnp.float32)
        upper_sum = jnp.zeros((midpoint_entries, D), jnp.float32)
        lower_sum = jnp.zeros((midpoint_entries, D), jnp.float32)
        for rotation in range(STEPS):
            above_adjacent_picture_vectors = image_units[(block_index + rotation) % BLOCKS]
            below_adjacent_picture_vectors = image_units[(block_index - rotation) % BLOCKS]
            above_label_polarity = first_labels[:, :midpoint_entries] if rotation == 0 else -1.0
            below_label_polarity = first_labels[:, midpoint_entries:] if rotation == 0 else -1.0
            above_coupling_coefficient = sigmoid_cost_coefficients(cross_dot_products(above_adjacent_picture_vectors, device_text_vectors[:midpoint_entries], exponentiated_scale, rotation_offset), above_label_polarity, exponentiated_scale)
            below_coupling_coefficient = sigmoid_cost_coefficients(cross_dot_products(below_adjacent_picture_vectors, device_text_vectors[midpoint_entries:], exponentiated_scale, rotation_offset), below_label_polarity, exponentiated_scale)
            upper_sum = upper_sum + lax.dot_general(above_coupling_coefficient, above_adjacent_picture_vectors, (((0,), (0,)), ((), ())), preferred_element_type=jnp.float32)
            lower_sum = lower_sum + lax.dot_general(below_coupling_coefficient, below_adjacent_picture_vectors, (((0,), (0,)), ((), ())), preferred_element_type=jnp.float32)
        direction = jnp.concatenate([upper_sum, lower_sum], axis=0)
        unit_flat, inverse_norm = unit_rows(caption_blocks[block_index])
        return finish(unit_flat, inverse_norm, direction)
    block_ids = jnp.arange(BLOCKS, dtype=jnp.int32)
    image_grad = lax.map(image_block, block_ids).reshape(ROWS, D)
    caption_grad = lax.map(caption_block, block_ids).reshape(ROWS, D)
    return (image_grad, caption_grad)
```

```python
import functools

import jax
import jax.numpy as jnp
from jax import lax
from jax.experimental import pallas as pl
from jax.experimental.pallas import tpu as pltpu
from jax.sharding import PartitionSpec as P

CHUNKS = 3
NORM_ROWS = 32
MESH = pl.DeviceIdType.MESH

A0, A1, A2, A3, B0, B1, B2, B3 = range(8)
(
    OWN_A_PAIR,
    OWN_A_FAR,
    A1_FAR,
    A2_PAIR,
    OWN_B_FAR,
    B2_PAIR,
    SUM_B1,
    SUM_B3,
    SUM_A3,
    SUM_A1,
    SUM_A2,
    SUM_B2,
) = range(12)


def kernel(
    groups,
    total,
    image_hbm,
    text_hbm,
    position_hbm,
    exponent_ref,
    offset_ref,
    image_out,
    text_out,
    image_ref,
    text_ref,
    position_ref,
    image_unit,
    captions,
    coefs,
    partial,
    staged,
    returned,
    direction,
    image_inverse,
    text_inverse,
    load_sem,
    send_sem,
    recv_sem,
):
    rows, width = image_hbm.shape
    half = rows // 2
    chunk = half // CHUNKS
    me = lax.axis_index("blk") * groups + lax.axis_index("grp")
    parity = lax.rem(me, 2)
    step = 1 - 2 * parity

    def place(index):
        index = lax.rem(index + total, total)
        return (index // groups, lax.rem(index, groups))

    pair = place(me + step)
    ahead = place(me + 2 * step)
    behind = place(me - 2 * step)

    barrier = pltpu.get_barrier_semaphore()
    for device in (pair, ahead, behind):
        pl.semaphore_signal(barrier, inc=1, device_id=device, device_id_type=MESH)

    start_a = pl.multiple_of(parity * half, half)
    start_b = pl.multiple_of(half - parity * half, half)

    def load(n, source, target):
        return pltpu.make_async_copy(source, target, load_sem.at[n])

    half_a, half_b = (pl.ds(start_a, half), pl.ds(start_b, half))
    loads = (
        load(0, text_hbm.at[half_b], text_ref.at[half_b]),
        load(1, text_hbm.at[half_a], text_ref.at[half_a]),
        load(2, image_hbm, image_ref),
        load(3, position_hbm, position_ref),
    )
    for copy in loads:
        copy.start()

    def piece(c):
        return pl.ds(c * chunk, chunk)

    def message(name, c, source, target, device):
        return pltpu.make_async_remote_copy(
            src_ref=source.at[piece(c)],
            dst_ref=target.at[piece(c)],
            send_sem=send_sem.at[name, c],
            recv_sem=recv_sem.at[name, c],
            device_id=device,
            device_id_type=MESH,
        )

    routes = {
        OWN_A_PAIR: (captions.at[A0], captions.at[B1], pair),
        OWN_A_FAR: (captions.at[A0], captions.at[A2], ahead),
        A1_FAR: (captions.at[A1], captions.at[A3], ahead),
        A2_PAIR: (captions.at[A2], captions.at[B3], pair),
        OWN_B_FAR: (captions.at[B0], captions.at[B2], behind),
        B2_PAIR: (captions.at[B2], captions.at[A1], pair),
        SUM_B1: (staged.at[0], returned.at[0], pair),
        SUM_B3: (staged.at[1], returned.at[1], pair),
        SUM_A3: (staged.at[2], returned.at[2], behind),
        SUM_A1: (staged.at[3], returned.at[3], pair),
        SUM_A2: (staged.at[4], returned.at[4], behind),
        SUM_B2: (staged.at[5], returned.at[5], ahead),
    }

    def send(name, c):
        message(name, c, *routes[name]).start()

    def receive(name, c):
        message(name, c, *routes[name]).wait_recv()

    def normalize(source, inverse, slot_ref, source_start):
        def body(i, carry):
            at = pl.multiple_of(i * NORM_ROWS, NORM_ROWS)
            here = pl.ds(pl.multiple_of(source_start + at, NORM_ROWS), NORM_ROWS)
            values = source[here, :].astype(jnp.float32)
            scale = lax.rsqrt(jnp.sum(values * values, axis=1, keepdims=True) + 1e-06)
            inverse[here, :] = scale
            slot_ref[pl.ds(at, NORM_ROWS), :] = (values * scale).astype(jnp.bfloat16)
            return carry

        lax.fori_loop(0, slot_ref.shape[0] // NORM_ROWS, body, 0)

    loads[0].wait()
    normalize(text_ref, text_inverse, captions.at[B0], start_b)
    pl.semaphore_wait(barrier, 3)
    for c in range(CHUNKS):
        send(OWN_B_FAR, c)
    loads[1].wait()
    normalize(text_ref, text_inverse, captions.at[A0], start_a)
    send(OWN_A_PAIR, 0)
    send(OWN_A_FAR, 0)
    for load in loads[2:]:
        load.wait()
    normalize(image_ref, image_inverse, image_unit, 0)

    scale = jnp.exp(jnp.full((1, rows), exponent_ref[0], jnp.float32))
    offset = offset_ref[0]

    def tile(slot, c, first_row=None):
        text = captions[slot, piece(c), :]
        logit = (
            lax.dot_general(
                text,
                image_unit[...],
                (((1,), (1,)), ((), ())),
                preferred_element_type=jnp.float32,
            )
            * scale
            + offset
        )
        if first_row is None:
            coef = scale * jax.nn.sigmoid(logit)
        else:
            row = lax.broadcasted_iota(jnp.int32, logit.shape, 0) + first_row + c * chunk
            polarity = jnp.where(row == position_ref[0:1, :], 1.0, -1.0)
            coef = scale * (-polarity * jax.nn.sigmoid(-polarity * logit))
        coef = coef.astype(jnp.bfloat16)
        coefs[slot, piece(c), :] = coef
        return jnp.dot(coef, image_unit[...], preferred_element_type=jnp.float32)

    def relay(name, c, source, buffer, slot, part):
        receive(source, c)
        arrived = returned[buffer, piece(c), :].astype(jnp.float32)
        staged[slot, piece(c), :] = (arrived + partial[part, piece(c), :]).astype(
            jnp.bfloat16
        )
        send(name, c)

    tile_width = 384 if width % 384 == 0 else 128

    def accumulate(i, carry):
        lanes = pl.ds(pl.multiple_of(i * tile_width, 128), tile_width)
        result = jnp.zeros((rows, tile_width), jnp.float32)
        for slot in range(8):
            result += lax.dot_general(
                coefs[slot],
                captions[slot, :, lanes],
                (((0,), (0,)), ((), ())),
                preferred_element_type=jnp.float32,
            )
        direction[:, lanes] = result
        return carry

    def finish(source, inverse, here, value):
        scale = inverse[here, :]
        flat = source[here, :].astype(jnp.float32) * scale
        cosine = jnp.sum(flat * value, axis=1, keepdims=True)
        return (scale * (value - flat * cosine)).astype(jnp.bfloat16)

    def finish_images(i, carry):
        here = pl.ds(pl.multiple_of(i * NORM_ROWS, NORM_ROWS), NORM_ROWS)
        image_out[here, :] = finish(image_ref, image_inverse, here, direction[here, :])
        return carry


    def finish_text(c, start, part, buffers):
        def body(i, carry):
            at = pl.multiple_of(c * chunk + i * NORM_ROWS, NORM_ROWS)
            local = pl.ds(at, NORM_ROWS)
            here = pl.ds(pl.multiple_of(start + at, NORM_ROWS), NORM_ROWS)
            value = partial[part, local, :]
            for buffer in buffers:
                value += returned[buffer, local, :].astype(jnp.float32)
            text_out[here, :] = finish(text_ref, text_inverse, here, value)
            return carry

        lax.fori_loop(0, chunk // NORM_ROWS, body, 0)

    def forward(arrival, name, c):
        receive(arrival, c)
        send(name, c)

    def keep(slot, part, c, first_row=None):
        partial[part, piece(c), :] = tile(slot, c, first_row)

    def give(arrival, slot, stage, c):
        receive(arrival, c)
        staged[stage, piece(c), :] = tile(slot, c).astype(jnp.bfloat16)

    def images():
        lax.fori_loop(0, width // tile_width, accumulate, 0)
        lax.fori_loop(0, rows // NORM_ROWS, finish_images, 0)

    for c in range(CHUNKS):
        forward(OWN_B_FAR, B2_PAIR, c)
        if c + 1 < CHUNKS:
            send(OWN_A_FAR, c + 1)
            send(OWN_A_PAIR, c + 1)
    for c in range(CHUNKS):
        forward(B2_PAIR, A1_FAR, c)
        forward(OWN_A_FAR, A2_PAIR, c)
    give(OWN_A_PAIR, B1, 0, 0)
    send(SUM_B1, 0)
    for c in range(1, CHUNKS):
        give(OWN_A_PAIR, B1, 0, c)

    for c in range(CHUNKS):
        keep(A1, 0, c)
        give(A1_FAR, A3, 2, c)
        send(SUM_A3, c)
        give(A2_PAIR, B3, 1, c)
        send(SUM_B3, c)
    for c in range(CHUNKS):
        keep(A2, 1, c)
        keep(B2, 2, c)

    for c in range(CHUNKS):
        relay(SUM_A1, c, SUM_A3, 2, 3, 0)
        relay(SUM_A2, c, SUM_B3, 1, 4, 1)
    for c in range(1, CHUNKS):
        send(SUM_B1, c)

    for c in range(CHUNKS):
        keep(A0, 3, c, start_a)
        keep(B0, 4, c, start_b)

    for c in range(CHUNKS):
        relay(SUM_B2, c, SUM_A1, 3, 5, 2)

    images()

    for c in range(CHUNKS):
        receive(SUM_B1, c)
        receive(SUM_A2, c)
        finish_text(c, start_a, 3, (0, 4))
    for c in range(CHUNKS):
        receive(SUM_B2, c)
        finish_text(c, start_b, 4, (5,))

    for name in routes:
        for c in range(CHUNKS):
            message(name, c, *routes[name]).wait_send()


def store(image_grad, text_grad, image_out, text_out, sem):
    copies = (
        pltpu.make_async_copy(image_grad, image_out, sem.at[0]),
        pltpu.make_async_copy(text_grad, text_out, sem.at[1]),
    )
    for copy in copies:
        copy.start()
    for copy in copies:
        copy.wait()


def solution(mesh):
    groups = mesh.shape["grp"]
    total = mesh.shape["blk"] * groups

    def local(images, texts, positions, exponent, offset):
        rows, width = images.shape
        half = rows // 2
        vmem = pl.BlockSpec(memory_space=pltpu.VMEM)
        hbm = pl.BlockSpec(memory_space=pltpu.HBM)
        smem = pl.BlockSpec(memory_space=pltpu.SMEM)
        images, texts, positions = (
            pltpu.with_memory_space_constraint(x, pltpu.HBM) for x in (images, texts, positions)
        )
        grads = pl.pallas_call(
            functools.partial(kernel, groups, total),
            out_shape=(
                pltpu.VMEM((rows, width), jnp.bfloat16),
                pltpu.VMEM((rows, width), jnp.bfloat16),
            ),
            in_specs=[hbm, hbm, hbm, smem, smem],
            out_specs=(vmem, vmem),
            scratch_shapes=[
                pltpu.VMEM((rows, width), jnp.bfloat16),
                pltpu.VMEM((rows, width), jnp.bfloat16),
                pltpu.VMEM((1, rows), jnp.int32),
                pltpu.VMEM((rows, width), jnp.bfloat16),
                pltpu.VMEM((8, half, width), jnp.bfloat16),
                pltpu.VMEM((8, half, rows), jnp.bfloat16),
                pltpu.VMEM((5, half, width), jnp.float32),
                pltpu.VMEM((6, half, width), jnp.bfloat16),
                pltpu.VMEM((6, half, width), jnp.bfloat16),
                pltpu.VMEM((rows, width), jnp.float32),
                pltpu.VMEM((rows, 1), jnp.float32),
                pltpu.VMEM((rows, 1), jnp.float32),
                pltpu.SemaphoreType.DMA((4,)),
                pltpu.SemaphoreType.DMA((12, CHUNKS)),
                pltpu.SemaphoreType.DMA((12, CHUNKS)),
            ],
            compiler_params=pltpu.CompilerParams(
                collective_id=0, has_side_effects=True, vmem_limit_bytes=24 * 1024 * 1024
            ),
        )(images, texts, positions, exponent, offset)
        grads = tuple(pltpu.with_memory_space_constraint(g, pltpu.VMEM) for g in grads)
        return pl.pallas_call(
            store,
            out_shape=(jax.ShapeDtypeStruct((rows, width), jnp.bfloat16),) * 2,
            in_specs=[vmem, vmem],
            out_specs=(hbm, hbm),
            scratch_shapes=[pltpu.SemaphoreType.DMA((2,))],
        )(*grads)

    shard = P(("blk", "grp"), None)
    return jax.shard_map(
        local,
        mesh=mesh,
        in_specs=(shard, shard, shard, P(), P()),
        out_specs=(shard, shard),
        check_vma=False,
    )
```

```python
import functools

import jax
import jax.numpy as jnp
from jax import lax
from jax.experimental import pallas as pl
from jax.experimental.pallas import tpu as pltpu
from jax.sharding import PartitionSpec as P

CHUNKS = 3
NORM_ROWS = 32
MESH = pl.DeviceIdType.MESH

F0, F1, F2, N0, N1 = range(5)
OWN_F0, OWN_F1, OWN_N0, OWN_N1, PAIR_F1, PAIR_F2, PAIR_N0, PAIR_N1 = range(8)
FAR, HOP, NEAR, SUM_F2, SUM_F1, SUM_N1, IMAGE, SUM_IMAGE = range(8)


def kernel(
    groups,
    total,
    image_hbm,
    text_hbm,
    position_hbm,
    exponent_ref,
    offset_ref,
    image_out,
    text_out,
    image_ref,
    text_ref,
    position_ref,
    image_unit,
    pair_unit,
    captions,
    coefs,
    partial,
    staged,
    returned,
    image_staged,
    image_returned,
    direction,
    image_inverse,
    text_inverse,
    load_sem,
    send_sem,
    recv_sem,
):
    rows, width = image_hbm.shape
    half = rows // 2
    chunk, band = half // CHUNKS, rows // CHUNKS
    me = lax.axis_index("blk") * groups + lax.axis_index("grp")
    parity = lax.rem(me, 2)
    reach = 4 * parity - 2

    def place(index):
        index = lax.rem(index + total, total)
        return (index // groups, lax.rem(index, groups))

    pair = place(me + 1 - 2 * parity)
    far = place(me + reach)
    near = place(me - reach)

    barrier = pltpu.get_barrier_semaphore()
    for device in (pair, far, near):
        pl.semaphore_signal(barrier, inc=1, device_id=device, device_id_type=MESH)

    start_f = pl.multiple_of(half - parity * half, half)
    start_n = pl.multiple_of(parity * half, half)

    def load(n, source, target):
        return pltpu.make_async_copy(source, target, load_sem.at[n])

    half_f, half_n = (pl.ds(start_f, half), pl.ds(start_n, half))
    loads = (
        load(0, text_hbm.at[half_f], text_ref.at[half_f]),
        load(1, text_hbm.at[half_n], text_ref.at[half_n]),
        load(2, image_hbm, image_ref),
        load(3, position_hbm, position_ref),
    )
    for copy in loads:
        copy.start()

    def piece(c):
        return pl.ds(c * chunk, chunk)

    def stripe(c):
        return pl.ds(c * band, band)

    routes = {
        FAR: (captions.at[F0], captions.at[F1], far, piece),
        HOP: (captions.at[F1], captions.at[F2], far, piece),
        NEAR: (captions.at[N0], captions.at[N1], near, piece),
        SUM_F2: (staged.at[0], returned.at[0], near, piece),
        SUM_F1: (staged.at[1], returned.at[1], near, piece),
        SUM_N1: (staged.at[2], returned.at[2], far, piece),
        IMAGE: (image_unit, pair_unit, pair, stripe),
        SUM_IMAGE: (image_staged, image_returned, pair, stripe),
    }

    def message(name, c):
        source, target, device, part = routes[name]
        return pltpu.make_async_remote_copy(
            src_ref=source.at[part(c)],
            dst_ref=target.at[part(c)],
            send_sem=send_sem.at[name, c],
            recv_sem=recv_sem.at[name, c],
            device_id=device,
            device_id_type=MESH,
        )

    def send(name, c):
        message(name, c).start()

    def receive(name, c):
        message(name, c).wait_recv()

    def normalize(source, inverse, target, source_start):
        def body(i, carry):
            at = pl.multiple_of(i * NORM_ROWS, NORM_ROWS)
            here = pl.ds(pl.multiple_of(source_start + at, NORM_ROWS), NORM_ROWS)
            values = source[here, :].astype(jnp.float32)
            scale = lax.rsqrt(jnp.sum(values * values, axis=1, keepdims=True) + 1e-06)
            inverse[here, :] = scale
            target[pl.ds(at, NORM_ROWS), :] = (values * scale).astype(jnp.bfloat16)
            return carry

        lax.fori_loop(0, target.shape[0] // NORM_ROWS, body, 0)

    loads[0].wait()
    normalize(text_ref, text_inverse, captions.at[F0], start_f)
    pl.semaphore_wait(barrier, 3)
    for c in range(CHUNKS):
        send(FAR, c)
    loads[1].wait()
    normalize(text_ref, text_inverse, captions.at[N0], start_n)
    for c in range(CHUNKS):
        send(NEAR, c)
    for copy in loads[2:]:
        copy.wait()
    normalize(image_ref, image_inverse, image_unit, 0)
    for c in range(CHUNKS):
        send(IMAGE, c)

    scale = jnp.exp(jnp.full((1, rows), exponent_ref[0], jnp.float32))
    offset = offset_ref[0]

    def tile(slot, images, table, c, first_row=None):
        text = captions[slot, piece(c), :]
        logit = (
            lax.dot_general(
                text,
                images[...],
                (((1,), (1,)), ((), ())),
                preferred_element_type=jnp.float32,
            )
            * scale
            + offset
        )
        if first_row is None:
            coef = scale * jax.nn.sigmoid(logit)
        else:
            row = lax.broadcasted_iota(jnp.int32, logit.shape, 0) + first_row + c * chunk
            polarity = jnp.where(row == position_ref[0:1, :], 1.0, -1.0)
            coef = scale * (-polarity * jax.nn.sigmoid(-polarity * logit))
        coef = coef.astype(jnp.bfloat16)
        coefs[table, piece(c), :] = coef
        return jnp.dot(coef, images[...], preferred_element_type=jnp.float32)

    def keep(part, c, value):
        partial[part, piece(c), :] = value

    def add(part, c, value):
        partial[part, piece(c), :] += value

    def give(stage, c, value):
        staged[stage, piece(c), :] = value.astype(jnp.bfloat16)

    def gather(c, terms):
        lanes = pl.ds(c * band, band)
        result = jnp.zeros((band, width), jnp.float32)
        for table, slot in terms:
            result += lax.dot_general(
                coefs[table, :, lanes],
                captions[slot],
                (((0,), (0,)), ((), ())),
                preferred_element_type=jnp.float32,
            )
        return result

    def finish(source, inverse, here, value):
        scale = inverse[here, :]
        flat = source[here, :].astype(jnp.float32) * scale
        cosine = jnp.sum(flat * value, axis=1, keepdims=True)
        return (scale * (value - flat * cosine)).astype(jnp.bfloat16)

    def finish_images(c):
        def body(i, carry):
            here = pl.ds(pl.multiple_of(c * band + i * NORM_ROWS, NORM_ROWS), NORM_ROWS)
            value = direction[here, :] + image_returned[here, :].astype(jnp.float32)
            image_out[here, :] = finish(image_ref, image_inverse, here, value)
            return carry

        lax.fori_loop(0, band // NORM_ROWS, body, 0)

    def finish_text(c, start, part, buffer):
        def body(i, carry):
            at = pl.multiple_of(c * chunk + i * NORM_ROWS, NORM_ROWS)
            local = pl.ds(at, NORM_ROWS)
            here = pl.ds(pl.multiple_of(start + at, NORM_ROWS), NORM_ROWS)
            value = partial[part, local, :] + returned[buffer, local, :].astype(jnp.float32)
            text_out[here, :] = finish(text_ref, text_inverse, here, value)
            return carry

        lax.fori_loop(0, chunk // NORM_ROWS, body, 0)

    for c in range(CHUNKS):
        keep(F0, c, tile(F0, image_unit, OWN_F0, c, start_f))
    for c in range(CHUNKS):
        receive(FAR, c)
        send(HOP, c)
        keep(N0, c, tile(N0, image_unit, OWN_N0, c, start_n))
    for c in range(CHUNKS):
        keep(F1, c, tile(F1, image_unit, OWN_F1, c))
    for c in range(CHUNKS):
        receive(NEAR, c)
        keep(N1, c, tile(N1, image_unit, OWN_N1, c))

    for c in range(CHUNKS):
        receive(IMAGE, c)
    for c in range(CHUNKS):
        give(2, c, partial[N1, piece(c), :] + tile(N1, pair_unit, PAIR_N1, c))
        send(SUM_N1, c)
    for c in range(CHUNKS):
        add(F1, c, tile(F1, pair_unit, PAIR_F1, c))
    for c in range(CHUNKS):
        receive(HOP, c)
        give(0, c, tile(F2, pair_unit, PAIR_F2, c))
        send(SUM_F2, c)
    for c in range(CHUNKS):
        add(N0, c, tile(N0, pair_unit, PAIR_N0, c))

    pair_terms = ((PAIR_F1, F1), (PAIR_F2, F2), (PAIR_N0, N0), (PAIR_N1, N1))
    for c in range(CHUNKS):
        image_staged[stripe(c), :] = gather(c, pair_terms).astype(jnp.bfloat16)
        send(SUM_IMAGE, c)

    for c in range(CHUNKS):
        receive(SUM_F2, c)
        arrived = returned[0, piece(c), :].astype(jnp.float32)
        give(1, c, arrived + partial[F1, piece(c), :])
        send(SUM_F1, c)

    own_terms = ((OWN_F0, F0), (OWN_F1, F1), (OWN_N0, N0), (OWN_N1, N1))
    for c in range(CHUNKS):
        direction[stripe(c), :] = gather(c, own_terms)
    for c in range(CHUNKS):
        receive(SUM_IMAGE, c)
        finish_images(c)
    for c in range(CHUNKS):
        receive(SUM_N1, c)
        finish_text(c, start_n, N0, 2)
    for c in range(CHUNKS):
        receive(SUM_F1, c)
        finish_text(c, start_f, F0, 1)

    for name in routes:
        for c in range(CHUNKS):
            message(name, c).wait_send()


def store(image_grad, text_grad, image_out, text_out, sem):
    copies = (
        pltpu.make_async_copy(image_grad, image_out, sem.at[0]),
        pltpu.make_async_copy(text_grad, text_out, sem.at[1]),
    )
    for copy in copies:
        copy.start()
    for copy in copies:
        copy.wait()


def solution(mesh):
    groups = mesh.shape["grp"]
    total = mesh.shape["blk"] * groups

    def local(images, texts, positions, exponent, offset):
        rows, width = images.shape
        half = rows // 2
        vmem = pl.BlockSpec(memory_space=pltpu.VMEM)
        hbm = pl.BlockSpec(memory_space=pltpu.HBM)
        smem = pl.BlockSpec(memory_space=pltpu.SMEM)
        images, texts, positions = (
            pltpu.with_memory_space_constraint(x, pltpu.HBM) for x in (images, texts, positions)
        )
        grads = pl.pallas_call(
            functools.partial(kernel, groups, total),
            out_shape=(
                pltpu.VMEM((rows, width), jnp.bfloat16),
                pltpu.VMEM((rows, width), jnp.bfloat16),
            ),
            in_specs=[hbm, hbm, hbm, smem, smem],
            out_specs=(vmem, vmem),
            scratch_shapes=[
                pltpu.VMEM((rows, width), jnp.bfloat16),
                pltpu.VMEM((rows, width), jnp.bfloat16),
                pltpu.VMEM((1, rows), jnp.int32),
                pltpu.VMEM((rows, width), jnp.bfloat16),
                pltpu.VMEM((rows, width), jnp.bfloat16),
                pltpu.VMEM((5, half, width), jnp.bfloat16),
                pltpu.VMEM((8, half, rows), jnp.bfloat16),
                pltpu.VMEM((5, half, width), jnp.float32),
                pltpu.VMEM((3, half, width), jnp.bfloat16),
                pltpu.VMEM((3, half, width), jnp.bfloat16),
                pltpu.VMEM((rows, width), jnp.bfloat16),
                pltpu.VMEM((rows, width), jnp.bfloat16),
                pltpu.VMEM((rows, width), jnp.float32),
                pltpu.VMEM((rows, 1), jnp.float32),
                pltpu.VMEM((rows, 1), jnp.float32),
                pltpu.SemaphoreType.DMA((4,)),
                pltpu.SemaphoreType.DMA((8, CHUNKS)),
                pltpu.SemaphoreType.DMA((8, CHUNKS)),
            ],
            compiler_params=pltpu.CompilerParams(
                collective_id=0, has_side_effects=True, vmem_limit_bytes=32 * 1024 * 1024
            ),
        )(images, texts, positions, exponent, offset)
        grads = tuple(pltpu.with_memory_space_constraint(g, pltpu.VMEM) for g in grads)
        return pl.pallas_call(
            store,
            out_shape=(jax.ShapeDtypeStruct((rows, width), jnp.bfloat16),) * 2,
            in_specs=[vmem, vmem],
            out_specs=(hbm, hbm),
            scratch_shapes=[pltpu.SemaphoreType.DMA((2,))],
        )(*grads)

    shard = P(("blk", "grp"), None)
    return jax.shard_map(
        local,
        mesh=mesh,
        in_specs=(shard, shard, shard, P(), P()),
        out_specs=(shard, shard),
        check_vma=False,
    )
```

```python
import functools

import jax
import jax.numpy as jnp
from jax import lax
from jax.experimental import pallas as pl
from jax.experimental.pallas import tpu as pltpu
from jax.sharding import PartitionSpec as P

CHUNKS = 3
NORM_ROWS = 64
MESH = pl.DeviceIdType.MESH

F0, F1, F2, N0, N1 = range(5)
OWN_F0, OWN_F1, OWN_N0, OWN_N1, PAIR_F1, PAIR_F2, PAIR_N0, PAIR_N1 = range(8)
IN_F1, IN_F2, IN_N1, IN_IMAGE, BACK_F2, BACK_F1, HOME, HOME_SPLIT, HOME_N, HOME_IMAGE = range(10)
(FAR, SPLIT, HOP, TURN, NEAR, IMAGE, SUM_F2, SUM_F1, SUM_N1, SUM_IMAGE) = range(10)

(
    UNIT_F,
    UNIT_N,
    UNIT_IMAGE,
    ENTER,
    READY,
    PUT_FAR,
    PUT_FAR_LOW,
    PUT_NEAR,
    PUT_NEAR_LOW,
    PUT_SPLIT,
    PUT_SPLIT_LOW,
    PUT_IMAGE,
    HOP_FIRST,
    HOP_LATER,
    TURN_BACK,
    TILE_F0,
    TILE_N0,
    TILE_F1,
    TILE_N1,
    CROSS_N0,
    CROSS_N1,
    CROSS_F1,
    CROSS_F2,
    PASS_F2,
    PASS_F1_FIRST,
    PASS_F1_LATER,
    GATHER_PAIR,
    GATHER_OWN,
    END_IMAGE,
    END_N,
    END_F,
) = range(31)

ORDER = (
    (UNIT_F, 0),
    (UNIT_F, 1),
    (ENTER, 0),
    (PUT_SPLIT, 0),
    (PUT_FAR, 0),
    (PUT_FAR, 1),
    (UNIT_IMAGE, 0),
    (UNIT_N, 0),
    (UNIT_N, 1),
    (UNIT_N, 2),
    (UNIT_IMAGE, 1),
    (PUT_IMAGE, 0),
    (UNIT_F, 2),
    (PUT_NEAR, 0),
    (PUT_FAR, 2),
    (READY, 0),
    (UNIT_IMAGE, 2),
    (HOP_LATER, 0),
    (PUT_SPLIT_LOW, 0),
    (PUT_NEAR_LOW, 0),
    (PUT_NEAR, 1),
    (PUT_NEAR_LOW, 1),
    (HOP_FIRST, 0),
    (PUT_SPLIT, 1),
    (PUT_IMAGE, 1),
    (HOP_FIRST, 1),
    (PUT_NEAR_LOW, 2),
    (TURN_BACK, 0),
    (PUT_IMAGE, 2),
    (HOP_FIRST, 2),
    (PUT_FAR_LOW, 0),
    (PUT_FAR_LOW, 1),
    (PUT_FAR_LOW, 2),
    (PUT_SPLIT_LOW, 1),
    (PUT_SPLIT, 2),
    (TILE_F0, 0),
    (TURN_BACK, 1),
    (TURN_BACK, 2),
    (PUT_NEAR, 2),
    (HOP_LATER, 1),
    (TILE_F1, 0),
    (TILE_N0, 0),
    (PUT_SPLIT_LOW, 2),
    (CROSS_F1, 0),
    (CROSS_F2, 0),
    (TILE_F1, 1),
    (TILE_F1, 2),
    (HOP_LATER, 2),
    (CROSS_F1, 1),
    (CROSS_F1, 2),
    (TILE_N1, 0),
    (CROSS_N0, 0),
    (TILE_N1, 1),
    (CROSS_N1, 0),
    (PASS_F2, 0),
    (CROSS_F2, 1),
    (PASS_F2, 1),
    (PASS_F1_LATER, 0),
    (CROSS_F2, 2),
    (PASS_F2, 2),
    (CROSS_N1, 1),
    (TILE_N1, 2),
    (PASS_F1_FIRST, 0),
    (CROSS_N1, 2),
    (GATHER_PAIR, 0),
    (GATHER_OWN, 0),
    (GATHER_PAIR, 1),
    (GATHER_PAIR, 2),
    (PASS_F1_LATER, 1),
    (GATHER_OWN, 1),
    (END_F, 0),
    (END_N, 0),
    (PASS_F1_FIRST, 1),
    (PASS_F1_LATER, 2),
    (END_IMAGE, 0),
    (GATHER_OWN, 2),
    (PASS_F1_FIRST, 2),
    (END_IMAGE, 1),
    (END_N, 1),
    (END_F, 1),
    (END_IMAGE, 2),
    (END_N, 2),
    (END_F, 2),
)

SLOT_OF = {CROSS_N0: N0, CROSS_N1: N1, CROSS_F1: F1, CROSS_F2: F2}
CROSSES = tuple(SLOT_OF[name] for name, _ in ORDER if name in SLOT_OF)


def starts(one, other):
    return ORDER.index(one) < ORDER.index(other)


def kernel(
    groups,
    total,
    image_hbm,
    text_hbm,
    position_hbm,
    exponent_ref,
    offset_ref,
    image_out,
    text_out,
    image_ref,
    text_ref,
    position_ref,
    image_unit,
    pair_unit,
    captions,
    coefs,
    partial,
    staged,
    returned,
    image_staged,
    image_returned,
    direction,
    image_inverse,
    text_inverse,
    load_sem,
    send_sem,
    recv_sem,
    ready_sem,
):
    rows, width = image_hbm.shape
    half = rows // 2
    chunk, band = half // CHUNKS, rows // CHUNKS
    me = lax.axis_index("blk") * groups + lax.axis_index("grp")
    parity = lax.rem(me, 2)
    reach = 4 * parity - 2

    def place(index):
        index = lax.rem(index + total, total)
        return (index // groups, lax.rem(index, groups))

    pair = place(me + 1 - 2 * parity)
    far, far_two = place(me + reach), place(me + 2 * reach)
    near, near_two = place(me - reach), place(me - 2 * reach)

    line = groups // 2
    z = lax.axis_index("grp") // 2
    since = parity * z + (1 - parity) * (line - 1 - z)
    until = line - 1 - since

    even, odd = parity == 0, parity == 1
    first = (since == 1) & (until > 0)
    later = (since > 1) & (until > 0)

    below, below_two = place(me - 2), place(me - 4)
    above, above_two = place(me + 2), place(me + 4)
    barrier = pltpu.get_barrier_semaphore()

    def greet(sem, device):
        pl.semaphore_signal(sem, inc=1, device_id=device, device_id_type=MESH)

    greet(barrier, pair)
    greet(barrier, below)

    @pl.when(z < line - 1)
    def _():
        greet(barrier, above)

    @pl.when(z <= 1)
    def _():
        greet(barrier, below_two)

    def enter():
        for start in (False, True):
            for end in (False, True):

                @pl.when(((z == 0) == start) & ((z >= line - 2) == end))
                def _():
                    pl.semaphore_wait(barrier, 3 - start + end)

        @pl.when(z >= line - 2)
        def _():
            greet(ready_sem, above_two)

        @pl.when(z == line - 1)
        def _():
            greet(ready_sem, above)

    def ready():
        @pl.when(z == 0)
        def _():
            pl.semaphore_wait(ready_sem, 2)

        @pl.when(z == 1)
        def _():
            pl.semaphore_wait(ready_sem, 1)

    start_f = pl.multiple_of(half - parity * half, half)
    start_n = pl.multiple_of(parity * half, half)

    def load(n, source, target):
        return pltpu.make_async_copy(source, target, load_sem.at[n])

    half_f, half_n = (pl.ds(start_f, half), pl.ds(start_n, half))
    loads = (
        load(0, text_hbm.at[half_f], text_ref.at[half_f]),
        load(1, text_hbm.at[half_n], text_ref.at[half_n]),
        load(2, image_hbm, image_ref),
        load(3, position_hbm, position_ref),
    )
    for copy in loads:
        copy.start()

    def piece(c):
        return pl.ds(0, half) if c is None else pl.ds(c * chunk, chunk)

    def stripe(c):
        return pl.ds(c * band, band)

    def message(name, arrival, source, target, device, part, c):
        return pltpu.make_async_remote_copy(
            src_ref=source.at[part(c)],
            dst_ref=target.at[part(c)],
            send_sem=send_sem.at[name, c],
            recv_sem=recv_sem.at[arrival, c],
            device_id=device,
            device_id_type=MESH,
        )

    landing = {
        IN_F1: (captions.at[F1], piece),
        IN_F2: (captions.at[F2], piece),
        IN_N1: (captions.at[N1], piece),
        IN_IMAGE: (pair_unit, stripe),
        BACK_F2: (returned.at[0], piece),
        BACK_F1: (returned.at[1], piece),
        HOME: (returned.at[2], piece),
        HOME_SPLIT: (returned.at[3], piece),
        HOME_N: (returned.at[4], piece),
        HOME_IMAGE: (image_returned, stripe),
    }

    def send(name, arrival, source, device, c):
        target, part = landing[arrival]
        message(name, arrival, source, target, device, part, c).start()

    def receive(arrival, c):
        target, part = landing[arrival]
        message(0, arrival, target, target, pair, part, c).wait_recv()

    def sent(name, source, part):
        for c in range(CHUNKS):
            message(name, 0, source, source, pair, part, c).wait_send()

    def normalize(source, inverse, target, source_start, at, count):
        def body(i, carry):
            local = pl.multiple_of(at + i * NORM_ROWS, NORM_ROWS)
            here = pl.ds(pl.multiple_of(source_start + local, NORM_ROWS), NORM_ROWS)
            values = source[here, :].astype(jnp.float32)
            scale = lax.rsqrt(jnp.sum(values * values, axis=1, keepdims=True) + 1e-06)
            inverse[here, :] = scale
            target[pl.ds(local, NORM_ROWS), :] = (values * scale).astype(jnp.bfloat16)
            return carry

        lax.fori_loop(0, count // NORM_ROWS, body, 0)

    scale = jnp.exp(jnp.full((1, rows), exponent_ref[0], jnp.float32))
    offset = offset_ref[0]

    def tile(slot, images, table, c, first_row=None):
        here = piece(c)
        text = captions[slot, here, :]
        logit = (
            lax.dot_general(
                text,
                images[...],
                (((1,), (1,)), ((), ())),
                preferred_element_type=jnp.float32,
            )
            * scale
            + offset
        )
        if first_row is None:
            coef = scale * jax.nn.sigmoid(logit)
        else:
            row = lax.broadcasted_iota(jnp.int32, logit.shape, 0) + first_row + (c or 0) * chunk
            polarity = jnp.where(row == position_ref[0:1, :], 1.0, -1.0)
            coef = scale * (-polarity * jax.nn.sigmoid(-polarity * logit))
        coef = coef.astype(jnp.bfloat16)
        coefs[table, here, :] = coef
        return jnp.dot(coef, images[...], preferred_element_type=jnp.float32)

    def keep(part, c, value):
        partial[part, piece(c), :] = value

    def add(part, c, value):
        partial[part, piece(c), :] += value

    def give(stage, c, value):
        staged[stage, piece(c), :] = value.astype(jnp.bfloat16)

    def gather(c, terms):
        lanes = pl.ds(c * band, band)
        result = jnp.zeros((band, width), jnp.float32)
        for table, slot in terms:
            result += lax.dot_general(
                coefs[table, :, lanes],
                captions[slot],
                (((0,), (0,)), ((), ())),
                preferred_element_type=jnp.float32,
            )
        return result

    def finish(source, inverse, here, value):
        scale = inverse[here, :]
        flat = source[here, :].astype(jnp.float32) * scale
        cosine = jnp.sum(flat * value, axis=1, keepdims=True)
        return (scale * (value - flat * cosine)).astype(jnp.bfloat16)

    def finish_images(c):
        def body(i, carry):
            here = pl.ds(pl.multiple_of(c * band + i * NORM_ROWS, NORM_ROWS), NORM_ROWS)
            value = direction[here, :] + image_returned[here, :].astype(jnp.float32)
            image_out[here, :] = finish(image_ref, image_inverse, here, value)
            return carry

        lax.fori_loop(0, band // NORM_ROWS, body, 0)

    def finish_text(c, start, part, buffer):
        def body(i, carry):
            at = pl.multiple_of(c * chunk + i * NORM_ROWS, NORM_ROWS)
            local = pl.ds(at, NORM_ROWS)
            here = pl.ds(pl.multiple_of(start + at, NORM_ROWS), NORM_ROWS)
            value = partial[part, local, :] + returned[buffer, local, :].astype(jnp.float32)
            text_out[here, :] = finish(text_ref, text_inverse, here, value)
            return carry

        lax.fori_loop(0, chunk // NORM_ROWS, body, 0)

    def unit_f(c):
        if c == 0:
            loads[0].wait()
        normalize(text_ref, text_inverse, captions.at[F0], start_f, c * chunk, chunk)

    def unit_n(c):
        if c == 0:
            loads[1].wait()
        normalize(text_ref, text_inverse, captions.at[N0], start_n, c * chunk, chunk)

    def unit_image(c):
        if c == 0:
            loads[2].wait()
            loads[3].wait()
        normalize(image_ref, image_inverse, image_unit, 0, c * band, band)

    def put_far(low):
        def run(c):
            @pl.when((until == 0) & (even if low else odd))
            def _():
                send(FAR, IN_F2, captions.at[F0], far_two, c)

            if not low:
                @pl.when(until > 0)
                def _():
                    send(FAR, IN_F1, captions.at[F0], far, c)

        return run

    def put_split(low):
        def run(c):
            @pl.when((until == 1) & (even if low else odd))
            def _():
                send(SPLIT, IN_F2, captions.at[F0], far_two, c)

        return run

    def put_near(low):
        wraps = (since == 0) & odd

        def run(c):
            @pl.when(wraps if low else jnp.logical_not(wraps))
            def _():
                send(NEAR, IN_N1, captions.at[N0], near, c)

        return run

    def put_image(c):
        send(IMAGE, IN_IMAGE, image_unit, pair, c)

    def hop(condition, op):
        def run(c):
            @pl.when(condition)
            def _():
                if starts((op, c), (TILE_F1, c)):
                    receive(IN_F1, c)
                send(HOP, IN_F2, captions.at[F1], far, c)

        return run

    def turn_back(c):
        @pl.when(since == 1)
        def _():
            if starts((TURN_BACK, c), (CROSS_F2, c)):
                receive(IN_F2, c)
            send(TURN, IN_F1, captions.at[F2], near, c)

    def tile_f0(c):
        keep(F0, None, tile(F0, image_unit, OWN_F0, None, start_f))

    def tile_n0(c):
        keep(N0, None, tile(N0, image_unit, OWN_N0, None, start_n))

    def tile_f1(c):
        waits = (since == 0) | (until == 0)
        if not starts((HOP_FIRST, c), (TILE_F1, c)):
            waits = waits | first
        if not starts((HOP_LATER, c), (TILE_F1, c)):
            waits = waits | later

        @pl.when(waits)
        def _():
            receive(IN_F1, c)

        keep(F1, c, tile(F1, image_unit, OWN_F1, c))

    def tile_n1(c):
        receive(IN_N1, c)
        keep(N1, c, tile(N1, image_unit, OWN_N1, c))

    def cross(slot, table, c, whole=False):
        if (CROSSES[0], 0) == (slot, c):
            for i in range(CHUNKS):
                receive(IN_IMAGE, i)
        return tile(slot, pair_unit, table, None if whole else c)

    def cross_n0(c):
        add(N0, None, cross(N0, PAIR_N0, c, True))

    def cross_n1(c):
        give(2, c, partial[N1, piece(c), :] + cross(N1, PAIR_N1, c))
        send(SUM_N1, HOME_N, staged.at[2], far, c)

    def cross_f1(c):
        add(F1, c, cross(F1, PAIR_F1, c))

        @pl.when(since == 0)
        def _():
            give(1, c, partial[F1, piece(c), :])
            send(SUM_F1, BACK_F1, staged.at[1], far, c)

        @pl.when(until == 0)
        def _():
            give(1, c, partial[F1, piece(c), :])
            send(SUM_F1, HOME, staged.at[1], near, c)

    def cross_f2(c):
        waits = since != 1
        if not starts((TURN_BACK, c), (CROSS_F2, c)):
            waits = since >= 0

        @pl.when(waits)
        def _():
            receive(IN_F2, c)

        keep(F2, c, cross(F2, PAIR_F2, c))

        @pl.when(since == 0)
        def _():
            give(0, c, partial[F2, piece(c), :])
            send(SUM_F2, HOME_SPLIT, staged.at[0], near_two, c)

        @pl.when(since > 1)
        def _():
            give(0, c, partial[F2, piece(c), :])
            send(SUM_F2, BACK_F2, staged.at[0], near, c)

    def pass_f2(c):
        @pl.when(since == 1)
        def _():
            receive(BACK_F1, c)
            arrived = returned[1, piece(c), :].astype(jnp.float32)
            give(0, c, arrived + partial[F2, piece(c), :])
            send(SUM_F2, HOME, staged.at[0], near_two, c)

    def pass_f1(condition):
        def run(c):
            @pl.when(condition)
            def _():
                receive(BACK_F2, c)
                arrived = returned[0, piece(c), :].astype(jnp.float32)
                give(1, c, arrived + partial[F1, piece(c), :])
                send(SUM_F1, HOME, staged.at[1], near, c)

        return run

    pair_terms = ((PAIR_F1, F1), (PAIR_F2, F2), (PAIR_N0, N0), (PAIR_N1, N1))
    own_terms = ((OWN_F0, F0), (OWN_F1, F1), (OWN_N0, N0), (OWN_N1, N1))

    def gather_pair(c):
        image_staged[stripe(c), :] = gather(c, pair_terms).astype(jnp.bfloat16)
        send(SUM_IMAGE, HOME_IMAGE, image_staged, pair, c)

    def gather_own(c):
        direction[stripe(c), :] = gather(c, own_terms)

    def end_image(c):
        receive(HOME_IMAGE, c)
        finish_images(c)

    def end_n(c):
        receive(HOME_N, c)
        finish_text(c, start_n, N0, 4)

    def end_f(c):
        receive(HOME, c)

        @pl.when(until == 1)
        def _():
            receive(HOME_SPLIT, c)
            add(F0, c, returned[3, piece(c), :].astype(jnp.float32))

        finish_text(c, start_f, F0, 2)

    steps = {
        UNIT_F: unit_f,
        UNIT_N: unit_n,
        UNIT_IMAGE: unit_image,
        ENTER: lambda c: enter(),
        READY: lambda c: ready(),
        PUT_FAR: put_far(False),
        PUT_FAR_LOW: put_far(True),
        PUT_NEAR: put_near(False),
        PUT_NEAR_LOW: put_near(True),
        PUT_SPLIT: put_split(False),
        PUT_SPLIT_LOW: put_split(True),
        PUT_IMAGE: put_image,
        HOP_FIRST: hop(first, HOP_FIRST),
        HOP_LATER: hop(later, HOP_LATER),
        TURN_BACK: turn_back,
        TILE_F0: tile_f0,
        TILE_N0: tile_n0,
        TILE_F1: tile_f1,
        TILE_N1: tile_n1,
        CROSS_N0: cross_n0,
        CROSS_N1: cross_n1,
        CROSS_F1: cross_f1,
        CROSS_F2: cross_f2,
        PASS_F2: pass_f2,
        PASS_F1_FIRST: pass_f1(first),
        PASS_F1_LATER: pass_f1(later),
        GATHER_PAIR: gather_pair,
        GATHER_OWN: gather_own,
        END_IMAGE: end_image,
        END_N: end_n,
        END_F: end_f,
    }
    for name, c in ORDER:
        steps[name](c)

    sent(FAR, captions.at[F0], piece)
    sent(NEAR, captions.at[N0], piece)
    sent(IMAGE, image_unit, stripe)
    sent(SUM_F2, staged.at[0], piece)
    sent(SUM_F1, staged.at[1], piece)
    sent(SUM_N1, staged.at[2], piece)
    sent(SUM_IMAGE, image_staged, stripe)

    @pl.when(until == 1)
    def _():
        sent(SPLIT, captions.at[F0], piece)

    @pl.when((since > 0) & (until > 0))
    def _():
        sent(HOP, captions.at[F1], piece)

    @pl.when(since == 1)
    def _():
        sent(TURN, captions.at[F2], piece)


def store(image_grad, text_grad, image_out, text_out, sem):
    copies = (
        pltpu.make_async_copy(image_grad, image_out, sem.at[0]),
        pltpu.make_async_copy(text_grad, text_out, sem.at[1]),
    )
    for copy in copies:
        copy.start()
    for copy in copies:
        copy.wait()


def solution(mesh):
    groups = mesh.shape["grp"]
    total = mesh.shape["blk"] * groups

    def local(images, texts, positions, exponent, offset):
        rows, width = images.shape
        half = rows // 2
        vmem = pl.BlockSpec(memory_space=pltpu.VMEM)
        hbm = pl.BlockSpec(memory_space=pltpu.HBM)
        smem = pl.BlockSpec(memory_space=pltpu.SMEM)
        images, texts, positions = (
            pltpu.with_memory_space_constraint(x, pltpu.HBM) for x in (images, texts, positions)
        )
        grads = pl.pallas_call(
            functools.partial(kernel, groups, total),
            out_shape=(
                pltpu.VMEM((rows, width), jnp.bfloat16),
                pltpu.VMEM((rows, width), jnp.bfloat16),
            ),
            in_specs=[hbm, hbm, hbm, smem, smem],
            out_specs=(vmem, vmem),
            scratch_shapes=[
                pltpu.VMEM((rows, width), jnp.bfloat16),
                pltpu.VMEM((rows, width), jnp.bfloat16),
                pltpu.VMEM((1, rows), jnp.int32),
                pltpu.VMEM((rows, width), jnp.bfloat16),
                pltpu.VMEM((rows, width), jnp.bfloat16),
                pltpu.VMEM((5, half, width), jnp.bfloat16),
                pltpu.VMEM((8, half, rows), jnp.bfloat16),
                pltpu.VMEM((5, half, width), jnp.float32),
                pltpu.VMEM((3, half, width), jnp.bfloat16),
                pltpu.VMEM((5, half, width), jnp.bfloat16),
                pltpu.VMEM((rows, width), jnp.bfloat16),
                pltpu.VMEM((rows, width), jnp.bfloat16),
                pltpu.VMEM((rows, width), jnp.float32),
                pltpu.VMEM((rows, 1), jnp.float32),
                pltpu.VMEM((rows, 1), jnp.float32),
                pltpu.SemaphoreType.DMA((4,)),
                pltpu.SemaphoreType.DMA((10, CHUNKS)),
                pltpu.SemaphoreType.DMA((10, CHUNKS)),
                pltpu.SemaphoreType.REGULAR,
            ],
            compiler_params=pltpu.CompilerParams(
                collective_id=0, has_side_effects=True, vmem_limit_bytes=32 * 1024 * 1024
            ),
        )(images, texts, positions, exponent, offset)
        grads = tuple(pltpu.with_memory_space_constraint(g, pltpu.VMEM) for g in grads)
        return pl.pallas_call(
            store,
            out_shape=(jax.ShapeDtypeStruct((rows, width), jnp.bfloat16),) * 2,
            in_specs=[vmem, vmem],
            out_specs=(hbm, hbm),
            scratch_shapes=[pltpu.SemaphoreType.DMA((2,))],
        )(*grads)

    shard = P(("blk", "grp"), None)
    return jax.shard_map(
        local,
        mesh=mesh,
        in_specs=(shard, shard, shard, P(), P()),
        out_specs=(shard, shard),
        check_vma=False,
    )
```

```python
import functools

import jax
import jax.numpy as jnp
from jax import lax
from jax.experimental import pallas as pl
from jax.experimental.pallas import tpu as pltpu
from jax.sharding import PartitionSpec as P

CHUNKS = 3
NORM_ROWS = 64
MESH = pl.DeviceIdType.MESH

F0, F1, F2, N0, N1 = range(5)
OWN_F0, OWN_F1, OWN_N0, OWN_N1, PAIR_F1, PAIR_F2, PAIR_N0, PAIR_N1 = range(8)
IN_F1, IN_F2, IN_N1, IN_IMAGE, BACK_F2, BACK_F1, HOME, HOME_SPLIT, HOME_N, HOME_IMAGE = range(10)
(FAR, SPLIT, HOP, TURN, NEAR, IMAGE, SUM_F2, SUM_F1, SUM_N1, SUM_IMAGE) = range(10)

(
    UNIT_F,
    UNIT_N,
    UNIT_IMAGE,
    ENTER,
    READY,
    PUT_FAR,
    PUT_FAR_LOW,
    PUT_NEAR,
    PUT_NEAR_LOW,
    PUT_SPLIT,
    PUT_SPLIT_LOW,
    PUT_IMAGE,
    HOP_FIRST,
    HOP_LATER,
    TURN_BACK,
    TILE_F0,
    TILE_N0,
    TILE_F1,
    TILE_N1,
    CROSS_N0,
    CROSS_N1,
    CROSS_F1,
    CROSS_F2,
    PASS_F2,
    PASS_F1_FIRST,
    PASS_F1_LATER,
    GATHER_PAIR,
    GATHER_OWN,
    END_IMAGE,
    END_N,
    END_F,
) = range(31)

ORDER = (
    (UNIT_F, 0),
    (UNIT_F, 1),
    (UNIT_N, 0),
    (ENTER, 0),
    (PUT_SPLIT, 0),
    (PUT_FAR, 0),
    (PUT_FAR, 1),
    (PUT_NEAR, 0),
    (UNIT_IMAGE, 0),
    (UNIT_N, 1),
    (UNIT_N, 2),
    (UNIT_IMAGE, 1),
    (PUT_IMAGE, 0),
    (UNIT_F, 2),
    (PUT_FAR, 2),
    (READY, 0),
    (UNIT_IMAGE, 2),
    (HOP_LATER, 0),
    (PUT_SPLIT_LOW, 0),
    (PUT_NEAR_LOW, 0),
    (PUT_NEAR, 1),
    (PUT_NEAR_LOW, 1),
    (HOP_FIRST, 0),
    (PUT_SPLIT, 1),
    (PUT_IMAGE, 1),
    (HOP_FIRST, 1),
    (PUT_NEAR_LOW, 2),
    (TURN_BACK, 0),
    (PUT_IMAGE, 2),
    (HOP_FIRST, 2),
    (PUT_FAR_LOW, 0),
    (PUT_FAR_LOW, 1),
    (PUT_FAR_LOW, 2),
    (PUT_SPLIT_LOW, 1),
    (PUT_SPLIT, 2),
    (TILE_F0, 0),
    (TURN_BACK, 1),
    (TURN_BACK, 2),
    (PUT_NEAR, 2),
    (HOP_LATER, 1),
    (TILE_F1, 0),
    (TILE_N0, 0),
    (PUT_SPLIT_LOW, 2),
    (CROSS_F1, 0),
    (CROSS_F2, 0),
    (TILE_F1, 1),
    (TILE_F1, 2),
    (HOP_LATER, 2),
    (CROSS_F1, 1),
    (CROSS_F1, 2),
    (TILE_N1, 0),
    (CROSS_N0, 0),
    (TILE_N1, 1),
    (CROSS_N1, 0),
    (PASS_F2, 0),
    (CROSS_F2, 1),
    (PASS_F2, 1),
    (PASS_F1_LATER, 0),
    (CROSS_F2, 2),
    (PASS_F2, 2),
    (CROSS_N1, 1),
    (TILE_N1, 2),
    (PASS_F1_FIRST, 0),
    (CROSS_N1, 2),
    (GATHER_PAIR, 0),
    (GATHER_OWN, 0),
    (GATHER_PAIR, 1),
    (GATHER_PAIR, 2),
    (PASS_F1_LATER, 1),
    (GATHER_OWN, 1),
    (END_F, 0),
    (END_N, 0),
    (PASS_F1_FIRST, 1),
    (PASS_F1_LATER, 2),
    (GATHER_OWN, 2),
    (END_IMAGE, 0),
    (PASS_F1_FIRST, 2),
    (END_IMAGE, 1),
    (END_IMAGE, 2),
    (END_N, 1),
    (END_F, 1),
    (END_N, 2),
    (END_F, 2),
)

SLOT_OF = {CROSS_N0: N0, CROSS_N1: N1, CROSS_F1: F1, CROSS_F2: F2}
CROSSES = tuple(SLOT_OF[name] for name, _ in ORDER if name in SLOT_OF)


def starts(one, other):
    return ORDER.index(one) < ORDER.index(other)


def kernel(
    groups,
    total,
    image_hbm,
    text_hbm,
    position_hbm,
    exponent_ref,
    offset_ref,
    image_out,
    text_out,
    image_ref,
    text_ref,
    position_ref,
    image_unit,
    pair_unit,
    captions,
    coefs,
    partial,
    staged,
    returned,
    image_staged,
    image_returned,
    direction,
    image_inverse,
    text_inverse,
    load_sem,
    send_sem,
    recv_sem,
    ready_sem,
):
    rows, width = image_hbm.shape
    half = rows // 2
    chunk, band = half // CHUNKS, rows // CHUNKS
    me = lax.axis_index("blk") * groups + lax.axis_index("grp")
    parity = lax.rem(me, 2)
    reach = 4 * parity - 2

    def place(index):
        index = lax.rem(index + total, total)
        return (index // groups, lax.rem(index, groups))

    pair = place(me + 1 - 2 * parity)
    far, far_two = place(me + reach), place(me + 2 * reach)
    near, near_two = place(me - reach), place(me - 2 * reach)

    line = groups // 2
    z = lax.axis_index("grp") // 2
    since = parity * z + (1 - parity) * (line - 1 - z)
    until = line - 1 - since

    even, odd = parity == 0, parity == 1
    first = (since == 1) & (until > 0)
    later = (since > 1) & (until > 0)

    below, below_two = place(me - 2), place(me - 4)
    above, above_two = place(me + 2), place(me + 4)
    barrier = pltpu.get_barrier_semaphore()

    def greet(sem, device):
        pl.semaphore_signal(sem, inc=1, device_id=device, device_id_type=MESH)

    greet(barrier, pair)
    greet(barrier, below)

    @pl.when(z < line - 1)
    def _():
        greet(barrier, above)

    @pl.when(z <= 1)
    def _():
        greet(barrier, below_two)

    def enter():
        for start in (False, True):
            for end in (False, True):

                @pl.when(((z == 0) == start) & ((z >= line - 2) == end))
                def _():
                    pl.semaphore_wait(barrier, 3 - start + end)

        @pl.when(z >= line - 2)
        def _():
            greet(ready_sem, above_two)

        @pl.when(z == line - 1)
        def _():
            greet(ready_sem, above)

    def ready():
        @pl.when(z == 0)
        def _():
            pl.semaphore_wait(ready_sem, 2)

        @pl.when(z == 1)
        def _():
            pl.semaphore_wait(ready_sem, 1)

    start_f = pl.multiple_of(half - parity * half, half)
    start_n = pl.multiple_of(parity * half, half)

    def load(n, source, target):
        return pltpu.make_async_copy(source, target, load_sem.at[n])

    half_f, half_n = (pl.ds(start_f, half), pl.ds(start_n, half))
    loads = (
        load(0, text_hbm.at[half_f], text_ref.at[half_f]),
        load(1, text_hbm.at[half_n], text_ref.at[half_n]),
        load(2, image_hbm, image_ref),
        load(3, position_hbm, position_ref),
    )
    for copy in loads:
        copy.start()

    def piece(c):
        return pl.ds(0, half) if c is None else pl.ds(c * chunk, chunk)

    def stripe(c):
        return pl.ds(c * band, band)

    def message(name, arrival, source, target, device, part, c):
        return pltpu.make_async_remote_copy(
            src_ref=source.at[part(c)],
            dst_ref=target.at[part(c)],
            send_sem=send_sem.at[name, c],
            recv_sem=recv_sem.at[arrival, c],
            device_id=device,
            device_id_type=MESH,
        )

    landing = {
        IN_F1: (captions.at[F1], piece),
        IN_F2: (captions.at[F2], piece),
        IN_N1: (captions.at[N1], piece),
        IN_IMAGE: (pair_unit, stripe),
        BACK_F2: (returned.at[0], piece),
        BACK_F1: (returned.at[1], piece),
        HOME: (returned.at[2], piece),
        HOME_SPLIT: (returned.at[3], piece),
        HOME_N: (returned.at[4], piece),
        HOME_IMAGE: (image_returned, stripe),
    }

    def send(name, arrival, source, device, c):
        target, part = landing[arrival]
        message(name, arrival, source, target, device, part, c).start()

    def receive(arrival, c):
        target, part = landing[arrival]
        message(0, arrival, target, target, pair, part, c).wait_recv()

    def sent(name, source, part):
        for c in range(CHUNKS):
            message(name, 0, source, source, pair, part, c).wait_send()

    def normalize(source, inverse, target, source_start, at, count):
        def body(i, carry):
            local = pl.multiple_of(at + i * NORM_ROWS, NORM_ROWS)
            here = pl.ds(pl.multiple_of(source_start + local, NORM_ROWS), NORM_ROWS)
            values = source[here, :].astype(jnp.float32)
            scale = lax.rsqrt(jnp.sum(values * values, axis=1, keepdims=True) + 1e-06)
            inverse[here, :] = scale
            target[pl.ds(local, NORM_ROWS), :] = (values * scale).astype(jnp.bfloat16)
            return carry

        lax.fori_loop(0, count // NORM_ROWS, body, 0)

    scale = jnp.exp(jnp.full((1, rows), exponent_ref[0], jnp.float32))
    offset = offset_ref[0]

    def tile(slot, images, table, c, first_row=None):
        here = piece(c)
        text = captions[slot, here, :]
        logit = (
            lax.dot_general(
                text,
                images[...],
                (((1,), (1,)), ((), ())),
                preferred_element_type=jnp.float32,
            )
            * scale
            + offset
        )
        if first_row is None:
            coef = scale * jax.nn.sigmoid(logit)
        else:
            row = lax.broadcasted_iota(jnp.int32, logit.shape, 0) + first_row + (c or 0) * chunk
            polarity = jnp.where(row == position_ref[0:1, :], 1.0, -1.0)
            coef = scale * (-polarity * jax.nn.sigmoid(-polarity * logit))
        coef = coef.astype(jnp.bfloat16)
        coefs[table, here, :] = coef
        return jnp.dot(coef, images[...], preferred_element_type=jnp.float32)

    def keep(part, c, value):
        partial[part, piece(c), :] = value

    def add(part, c, value):
        partial[part, piece(c), :] += value

    def give(stage, c, value):
        staged[stage, piece(c), :] = value.astype(jnp.bfloat16)

    def gather(c, terms):
        lanes = pl.ds(c * band, band)
        result = jnp.zeros((band, width), jnp.float32)
        for table, slot in terms:
            result += lax.dot_general(
                coefs[table, :, lanes],
                captions[slot],
                (((0,), (0,)), ((), ())),
                preferred_element_type=jnp.float32,
            )
        return result

    def finish(source, inverse, here, value):
        scale = inverse[here, :]
        flat = source[here, :].astype(jnp.float32) * scale
        cosine = jnp.sum(flat * value, axis=1, keepdims=True)
        return (scale * (value - flat * cosine)).astype(jnp.bfloat16)

    def finish_images(c):
        def body(i, carry):
            here = pl.ds(pl.multiple_of(c * band + i * NORM_ROWS, NORM_ROWS), NORM_ROWS)
            value = direction[here, :] + image_returned[here, :].astype(jnp.float32)
            image_out[here, :] = finish(image_ref, image_inverse, here, value)
            return carry

        lax.fori_loop(0, band // NORM_ROWS, body, 0)

    def finish_text(c, start, part, buffer):
        def body(i, carry):
            at = pl.multiple_of(c * chunk + i * NORM_ROWS, NORM_ROWS)
            local = pl.ds(at, NORM_ROWS)
            here = pl.ds(pl.multiple_of(start + at, NORM_ROWS), NORM_ROWS)
            value = partial[part, local, :] + returned[buffer, local, :].astype(jnp.float32)
            text_out[here, :] = finish(text_ref, text_inverse, here, value)
            return carry

        lax.fori_loop(0, chunk // NORM_ROWS, body, 0)

    def unit_f(c):
        if c == 0:
            loads[0].wait()
        normalize(text_ref, text_inverse, captions.at[F0], start_f, c * chunk, chunk)

    def unit_n(c):
        if c == 0:
            loads[1].wait()
        normalize(text_ref, text_inverse, captions.at[N0], start_n, c * chunk, chunk)

    def unit_image(c):
        if c == 0:
            loads[2].wait()
            loads[3].wait()
        normalize(image_ref, image_inverse, image_unit, 0, c * band, band)

    def put_far(low):
        def run(c):
            @pl.when((until == 0) & (even if low else odd))
            def _():
                send(FAR, IN_F2, captions.at[F0], far_two, c)

            if not low:
                @pl.when(until > 0)
                def _():
                    send(FAR, IN_F1, captions.at[F0], far, c)

        return run

    def put_split(low):
        def run(c):
            @pl.when((until == 1) & (even if low else odd))
            def _():
                send(SPLIT, IN_F2, captions.at[F0], far_two, c)

        return run

    def put_near(low):
        wraps = (since == 0) & odd

        def run(c):
            @pl.when(wraps if low else jnp.logical_not(wraps))
            def _():
                send(NEAR, IN_N1, captions.at[N0], near, c)

        return run

    def put_image(c):
        send(IMAGE, IN_IMAGE, image_unit, pair, c)

    def hop(condition, op):
        def run(c):
            @pl.when(condition)
            def _():
                if starts((op, c), (TILE_F1, c)):
                    receive(IN_F1, c)
                send(HOP, IN_F2, captions.at[F1], far, c)

        return run

    def turn_back(c):
        @pl.when(since == 1)
        def _():
            if starts((TURN_BACK, c), (CROSS_F2, c)):
                receive(IN_F2, c)
            send(TURN, IN_F1, captions.at[F2], near, c)

    def tile_f0(c):
        keep(F0, None, tile(F0, image_unit, OWN_F0, None, start_f))

    def tile_n0(c):
        keep(N0, None, tile(N0, image_unit, OWN_N0, None, start_n))

    def tile_f1(c):
        waits = (since == 0) | (until == 0)
        if not starts((HOP_FIRST, c), (TILE_F1, c)):
            waits = waits | first
        if not starts((HOP_LATER, c), (TILE_F1, c)):
            waits = waits | later

        @pl.when(waits)
        def _():
            receive(IN_F1, c)

        keep(F1, c, tile(F1, image_unit, OWN_F1, c))

    def tile_n1(c):
        receive(IN_N1, c)
        keep(N1, c, tile(N1, image_unit, OWN_N1, c))

    def cross(slot, table, c, whole=False):
        if (CROSSES[0], 0) == (slot, c):
            for i in range(CHUNKS):
                receive(IN_IMAGE, i)
        return tile(slot, pair_unit, table, None if whole else c)

    def cross_n0(c):
        add(N0, None, cross(N0, PAIR_N0, c, True))

    def cross_n1(c):
        give(2, c, partial[N1, piece(c), :] + cross(N1, PAIR_N1, c))
        send(SUM_N1, HOME_N, staged.at[2], far, c)

    def cross_f1(c):
        add(F1, c, cross(F1, PAIR_F1, c))

        @pl.when(since == 0)
        def _():
            give(1, c, partial[F1, piece(c), :])
            send(SUM_F1, BACK_F1, staged.at[1], far, c)

        @pl.when(until == 0)
        def _():
            give(1, c, partial[F1, piece(c), :])
            send(SUM_F1, HOME, staged.at[1], near, c)

    def cross_f2(c):
        waits = since != 1
        if not starts((TURN_BACK, c), (CROSS_F2, c)):
            waits = since >= 0

        @pl.when(waits)
        def _():
            receive(IN_F2, c)

        keep(F2, c, cross(F2, PAIR_F2, c))

        @pl.when(since == 0)
        def _():
            give(0, c, partial[F2, piece(c), :])
            send(SUM_F2, HOME_SPLIT, staged.at[0], near_two, c)

        @pl.when(since > 1)
        def _():
            give(0, c, partial[F2, piece(c), :])
            send(SUM_F2, BACK_F2, staged.at[0], near, c)

    def pass_f2(c):
        @pl.when(since == 1)
        def _():
            receive(BACK_F1, c)
            arrived = returned[1, piece(c), :].astype(jnp.float32)
            give(0, c, arrived + partial[F2, piece(c), :])
            send(SUM_F2, HOME, staged.at[0], near_two, c)

    def pass_f1(condition):
        def run(c):
            @pl.when(condition)
            def _():
                receive(BACK_F2, c)
                arrived = returned[0, piece(c), :].astype(jnp.float32)
                give(1, c, arrived + partial[F1, piece(c), :])
                send(SUM_F1, HOME, staged.at[1], near, c)

        return run

    pair_terms = ((PAIR_F1, F1), (PAIR_F2, F2), (PAIR_N0, N0), (PAIR_N1, N1))
    own_terms = ((OWN_F0, F0), (OWN_F1, F1), (OWN_N0, N0), (OWN_N1, N1))

    def gather_pair(c):
        image_staged[stripe(c), :] = gather(c, pair_terms).astype(jnp.bfloat16)
        send(SUM_IMAGE, HOME_IMAGE, image_staged, pair, c)

    def gather_own(c):
        direction[stripe(c), :] = gather(c, own_terms)

    def end_image(c):
        receive(HOME_IMAGE, c)
        finish_images(c)

    def end_n(c):
        receive(HOME_N, c)
        finish_text(c, start_n, N0, 4)

    def end_f(c):
        receive(HOME, c)

        @pl.when(until == 1)
        def _():
            receive(HOME_SPLIT, c)
            add(F0, c, returned[3, piece(c), :].astype(jnp.float32))

        finish_text(c, start_f, F0, 2)

    steps = {
        UNIT_F: unit_f,
        UNIT_N: unit_n,
        UNIT_IMAGE: unit_image,
        ENTER: lambda c: enter(),
        READY: lambda c: ready(),
        PUT_FAR: put_far(False),
        PUT_FAR_LOW: put_far(True),
        PUT_NEAR: put_near(False),
        PUT_NEAR_LOW: put_near(True),
        PUT_SPLIT: put_split(False),
        PUT_SPLIT_LOW: put_split(True),
        PUT_IMAGE: put_image,
        HOP_FIRST: hop(first, HOP_FIRST),
        HOP_LATER: hop(later, HOP_LATER),
        TURN_BACK: turn_back,
        TILE_F0: tile_f0,
        TILE_N0: tile_n0,
        TILE_F1: tile_f1,
        TILE_N1: tile_n1,
        CROSS_N0: cross_n0,
        CROSS_N1: cross_n1,
        CROSS_F1: cross_f1,
        CROSS_F2: cross_f2,
        PASS_F2: pass_f2,
        PASS_F1_FIRST: pass_f1(first),
        PASS_F1_LATER: pass_f1(later),
        GATHER_PAIR: gather_pair,
        GATHER_OWN: gather_own,
        END_IMAGE: end_image,
        END_N: end_n,
        END_F: end_f,
    }
    for name, c in ORDER:
        steps[name](c)

    sent(FAR, captions.at[F0], piece)
    sent(NEAR, captions.at[N0], piece)
    sent(IMAGE, image_unit, stripe)
    sent(SUM_F2, staged.at[0], piece)
    sent(SUM_F1, staged.at[1], piece)
    sent(SUM_N1, staged.at[2], piece)
    sent(SUM_IMAGE, image_staged, stripe)

    @pl.when(until == 1)
    def _():
        sent(SPLIT, captions.at[F0], piece)

    @pl.when((since > 0) & (until > 0))
    def _():
        sent(HOP, captions.at[F1], piece)

    @pl.when(since == 1)
    def _():
        sent(TURN, captions.at[F2], piece)


def store(image_grad, text_grad, image_out, text_out, sem):
    copies = (
        pltpu.make_async_copy(image_grad, image_out, sem.at[0]),
        pltpu.make_async_copy(text_grad, text_out, sem.at[1]),
    )
    for copy in copies:
        copy.start()
    for copy in copies:
        copy.wait()


def solution(mesh):
    groups = mesh.shape["grp"]
    total = mesh.shape["blk"] * groups

    def local(images, texts, positions, exponent, offset):
        rows, width = images.shape
        half = rows // 2
        vmem = pl.BlockSpec(memory_space=pltpu.VMEM)
        hbm = pl.BlockSpec(memory_space=pltpu.HBM)
        smem = pl.BlockSpec(memory_space=pltpu.SMEM)
        images, texts, positions = (
            pltpu.with_memory_space_constraint(x, pltpu.HBM) for x in (images, texts, positions)
        )
        grads = pl.pallas_call(
            functools.partial(kernel, groups, total),
            out_shape=(
                pltpu.VMEM((rows, width), jnp.bfloat16),
                pltpu.VMEM((rows, width), jnp.bfloat16),
            ),
            in_specs=[hbm, hbm, hbm, smem, smem],
            out_specs=(vmem, vmem),
            scratch_shapes=[
                pltpu.VMEM((rows, width), jnp.bfloat16),
                pltpu.VMEM((rows, width), jnp.bfloat16),
                pltpu.VMEM((1, rows), jnp.int32),
                pltpu.VMEM((rows, width), jnp.bfloat16),
                pltpu.VMEM((rows, width), jnp.bfloat16),
                pltpu.VMEM((5, half, width), jnp.bfloat16),
                pltpu.VMEM((8, half, rows), jnp.bfloat16),
                pltpu.VMEM((5, half, width), jnp.float32),
                pltpu.VMEM((3, half, width), jnp.bfloat16),
                pltpu.VMEM((5, half, width), jnp.bfloat16),
                pltpu.VMEM((rows, width), jnp.bfloat16),
                pltpu.VMEM((rows, width), jnp.bfloat16),
                pltpu.VMEM((rows, width), jnp.float32),
                pltpu.VMEM((rows, 1), jnp.float32),
                pltpu.VMEM((rows, 1), jnp.float32),
                pltpu.SemaphoreType.DMA((4,)),
                pltpu.SemaphoreType.DMA((10, CHUNKS)),
                pltpu.SemaphoreType.DMA((10, CHUNKS)),
                pltpu.SemaphoreType.REGULAR,
            ],
            compiler_params=pltpu.CompilerParams(
                collective_id=0, has_side_effects=True, vmem_limit_bytes=32 * 1024 * 1024
            ),
        )(images, texts, positions, exponent, offset)
        grads = tuple(pltpu.with_memory_space_constraint(g, pltpu.VMEM) for g in grads)
        return pl.pallas_call(
            store,
            out_shape=(jax.ShapeDtypeStruct((rows, width), jnp.bfloat16),) * 2,
            in_specs=[vmem, vmem],
            out_specs=(hbm, hbm),
            scratch_shapes=[pltpu.SemaphoreType.DMA((2,))],
        )(*grads)

    shard = P(("blk", "grp"), None)
    return jax.shard_map(
        local,
        mesh=mesh,
        in_specs=(shard, shard, shard, P(), P()),
        out_specs=(shard, shard),
        check_vma=False,
    )
```

```python
import functools

import jax
import jax.numpy as jnp
from jax import lax
from jax.experimental import pallas as pl
from jax.experimental.pallas import tpu as pltpu
from jax.sharding import PartitionSpec as P

CHUNKS = 3
NORM_ROWS = 64
MESH = pl.DeviceIdType.MESH

F0, F1, F2, N0, N1 = range(5)
OWN_F0, OWN_F1, OWN_N0, OWN_N1, PAIR_F1, PAIR_F2, PAIR_N0, PAIR_N1 = range(8)
IN_F1, IN_F2, IN_N1, IN_IMAGE, BACK_F2, BACK_F1, HOME, HOME_SPLIT, HOME_N, HOME_IMAGE = range(10)
(FAR, SPLIT, HOP, TURN, NEAR, IMAGE, SUM_F2, SUM_F1, SUM_N1, SUM_IMAGE) = range(10)

(
    UNIT_F,
    UNIT_N,
    UNIT_IMAGE,
    ENTER,
    READY,
    PUT_FAR,
    PUT_FAR_LOW,
    PUT_NEAR,
    PUT_NEAR_LOW,
    PUT_SPLIT,
    PUT_SPLIT_LOW,
    PUT_IMAGE,
    HOP_FIRST,
    HOP_LATER,
    TURN_BACK,
    TILE_F0,
    TILE_N0,
    TILE_F1,
    TILE_N1,
    CROSS_N0,
    CROSS_N1,
    CROSS_F1,
    CROSS_F2,
    PASS_F2,
    PASS_F1_FIRST,
    PASS_F1_LATER,
    GATHER_PAIR,
    GATHER_OWN,
    END_IMAGE,
    END_N,
    END_F,
) = range(31)

ORDER = (
    (UNIT_F, 0),
    (UNIT_F, 1),
    (ENTER, 0),
    (PUT_SPLIT, 0),
    (PUT_FAR, 0),
    (PUT_FAR, 1),
    (UNIT_IMAGE, 0),
    (UNIT_N, 0),
    (UNIT_N, 1),
    (UNIT_N, 2),
    (UNIT_IMAGE, 1),
    (PUT_IMAGE, 0),
    (UNIT_F, 2),
    (PUT_NEAR, 0),
    (PUT_FAR, 2),
    (READY, 0),
    (UNIT_IMAGE, 2),
    (HOP_LATER, 0),
    (PUT_SPLIT_LOW, 0),
    (PUT_NEAR_LOW, 0),
    (PUT_NEAR, 1),
    (PUT_NEAR_LOW, 1),
    (HOP_FIRST, 0),
    (PUT_SPLIT, 1),
    (PUT_IMAGE, 1),
    (HOP_FIRST, 1),
    (PUT_NEAR_LOW, 2),
    (TURN_BACK, 0),
    (PUT_IMAGE, 2),
    (HOP_FIRST, 2),
    (PUT_FAR_LOW, 0),
    (PUT_FAR_LOW, 1),
    (PUT_FAR_LOW, 2),
    (PUT_SPLIT_LOW, 1),
    (PUT_SPLIT, 2),
    (TILE_F0, 0),
    (TURN_BACK, 1),
    (TURN_BACK, 2),
    (PUT_NEAR, 2),
    (HOP_LATER, 1),
    (TILE_F1, 0),
    (TILE_N0, 0),
    (PUT_SPLIT_LOW, 2),
    (CROSS_F1, 0),
    (CROSS_F2, 0),
    (TILE_F1, 1),
    (TILE_F1, 2),
    (HOP_LATER, 2),
    (CROSS_F1, 1),
    (CROSS_F1, 2),
    (TILE_N1, 0),
    (CROSS_N0, 0),
    (TILE_N1, 1),
    (CROSS_N1, 0),
    (PASS_F2, 0),
    (CROSS_F2, 1),
    (PASS_F2, 1),
    (PASS_F1_LATER, 0),
    (CROSS_F2, 2),
    (PASS_F2, 2),
    (CROSS_N1, 1),
    (TILE_N1, 2),
    (PASS_F1_FIRST, 0),
    (CROSS_N1, 2),
    (GATHER_PAIR, 0),
    (GATHER_OWN, 0),
    (GATHER_PAIR, 1),
    (GATHER_PAIR, 2),
    (PASS_F1_LATER, 1),
    (GATHER_OWN, 1),
    (END_F, 0),
    (END_N, 0),
    (PASS_F1_FIRST, 1),
    (PASS_F1_LATER, 2),
    (END_IMAGE, 0),
    (GATHER_OWN, 2),
    (PASS_F1_FIRST, 2),
    (END_IMAGE, 1),
    (END_N, 1),
    (END_F, 1),
    (END_IMAGE, 2),
    (END_N, 2),
    (END_F, 2),
)

SLOT_OF = {CROSS_N0: N0, CROSS_N1: N1, CROSS_F1: F1, CROSS_F2: F2}
CROSSES = tuple(SLOT_OF[name] for name, _ in ORDER if name in SLOT_OF)


def starts(one, other):
    return ORDER.index(one) < ORDER.index(other)


def kernel(
    groups,
    total,
    image_hbm,
    text_hbm,
    position_hbm,
    exponent_ref,
    offset_ref,
    image_out,
    text_out,
    image_ref,
    text_ref,
    position_ref,
    image_unit,
    pair_unit,
    captions,
    coefs,
    partial,
    staged,
    returned,
    image_staged,
    image_returned,
    direction,
    image_inverse,
    text_inverse,
    load_sem,
    send_sem,
    recv_sem,
    ready_sem,
):
    rows, width = image_hbm.shape
    half = rows // 2
    chunk, band = half // CHUNKS, rows // CHUNKS
    me = lax.axis_index("blk") * groups + lax.axis_index("grp")
    parity = lax.rem(me, 2)
    reach = 4 * parity - 2

    def place(index):
        index = lax.rem(index + total, total)
        return (index // groups, lax.rem(index, groups))

    pair = place(me + 1 - 2 * parity)
    far, far_two = place(me + reach), place(me + 2 * reach)
    near, near_two = place(me - reach), place(me - 2 * reach)

    line = groups // 2
    z = lax.axis_index("grp") // 2
    since = parity * z + (1 - parity) * (line - 1 - z)
    until = line - 1 - since

    even, odd = parity == 0, parity == 1
    first = (since == 1) & (until > 0)
    later = (since > 1) & (until > 0)

    below, below_two = place(me - 2), place(me - 4)
    above, above_two = place(me + 2), place(me + 4)
    barrier = pltpu.get_barrier_semaphore()

    def greet(sem, device):
        pl.semaphore_signal(sem, inc=1, device_id=device, device_id_type=MESH)

    greet(barrier, pair)
    greet(barrier, below)

    @pl.when(z < line - 1)
    def _():
        greet(barrier, above)

    @pl.when(z <= 1)
    def _():
        greet(barrier, below_two)

    def enter():
        for start in (False, True):
            for end in (False, True):

                @pl.when(((z == 0) == start) & ((z >= line - 2) == end))
                def _():
                    pl.semaphore_wait(barrier, 3 - start + end)

        @pl.when(z >= line - 2)
        def _():
            greet(ready_sem, above_two)

        @pl.when(z == line - 1)
        def _():
            greet(ready_sem, above)

    def ready():
        @pl.when(z == 0)
        def _():
            pl.semaphore_wait(ready_sem, 2)

        @pl.when(z == 1)
        def _():
            pl.semaphore_wait(ready_sem, 1)

    start_f = pl.multiple_of(half - parity * half, half)
    start_n = pl.multiple_of(parity * half, half)

    def load(n, source, target):
        return pltpu.make_async_copy(source, target, load_sem.at[n])

    half_f, half_n = (pl.ds(start_f, half), pl.ds(start_n, half))
    loads = (
        load(0, text_hbm.at[half_f], text_ref.at[half_f]),
        load(1, text_hbm.at[half_n], text_ref.at[half_n]),
        load(2, image_hbm, image_ref),
        load(3, position_hbm, position_ref),
    )
    for copy in loads:
        copy.start()

    def piece(c):
        return pl.ds(0, half) if c is None else pl.ds(c * chunk, chunk)

    def stripe(c):
        return pl.ds(c * band, band)

    def message(name, arrival, source, target, device, part, c):
        return pltpu.make_async_remote_copy(
            src_ref=source.at[part(c)],
            dst_ref=target.at[part(c)],
            send_sem=send_sem.at[name, c],
            recv_sem=recv_sem.at[arrival, c],
            device_id=device,
            device_id_type=MESH,
        )

    landing = {
        IN_F1: (captions.at[F1], piece),
        IN_F2: (captions.at[F2], piece),
        IN_N1: (captions.at[N1], piece),
        IN_IMAGE: (pair_unit, stripe),
        BACK_F2: (returned.at[0], piece),
        BACK_F1: (returned.at[1], piece),
        HOME: (returned.at[2], piece),
        HOME_SPLIT: (returned.at[3], piece),
        HOME_N: (returned.at[4], piece),
        HOME_IMAGE: (image_returned, stripe),
    }

    def send(name, arrival, source, device, c):
        target, part = landing[arrival]
        message(name, arrival, source, target, device, part, c).start()

    def receive(arrival, c):
        target, part = landing[arrival]
        message(0, arrival, target, target, pair, part, c).wait_recv()

    def sent(name, source, part):
        for c in range(CHUNKS):
            message(name, 0, source, source, pair, part, c).wait_send()

    def normalize(source, inverse, target, source_start, at, count):
        def body(i, carry):
            local = pl.multiple_of(at + i * NORM_ROWS, NORM_ROWS)
            here = pl.ds(pl.multiple_of(source_start + local, NORM_ROWS), NORM_ROWS)
            values = source[here, :].astype(jnp.float32)
            scale = lax.rsqrt(jnp.sum(values * values, axis=1, keepdims=True) + 1e-06)
            inverse[here, :] = scale
            target[pl.ds(local, NORM_ROWS), :] = (values * scale).astype(jnp.bfloat16)
            return carry

        lax.fori_loop(0, count // NORM_ROWS, body, 0)

    scale = jnp.exp(jnp.full((1, rows), exponent_ref[0], jnp.float32))
    offset = offset_ref[0]

    def tile(slot, images, table, c, first_row=None):
        here = piece(c)
        text = captions[slot, here, :]
        logit = (
            lax.dot_general(
                text,
                images[...],
                (((1,), (1,)), ((), ())),
                preferred_element_type=jnp.float32,
            )
            * scale
            + offset
        )
        if first_row is None:
            coef = scale * jax.nn.sigmoid(logit)
        else:
            row = lax.broadcasted_iota(jnp.int32, logit.shape, 0) + first_row + (c or 0) * chunk
            polarity = jnp.where(row == position_ref[0:1, :], 1.0, -1.0)
            coef = scale * (-polarity * jax.nn.sigmoid(-polarity * logit))
        coef = coef.astype(jnp.bfloat16)
        coefs[table, here, :] = coef
        return jnp.dot(coef, images[...], preferred_element_type=jnp.float32)

    def keep(part, c, value):
        partial[part, piece(c), :] = value

    def add(part, c, value):
        partial[part, piece(c), :] += value

    def give(stage, c, value):
        staged[stage, piece(c), :] = value.astype(jnp.bfloat16)

    def gather(c, terms):
        lanes = pl.ds(c * band, band)
        result = jnp.zeros((band, width), jnp.float32)
        for table, slot in terms:
            result += lax.dot_general(
                coefs[table, :, lanes],
                captions[slot],
                (((0,), (0,)), ((), ())),
                preferred_element_type=jnp.float32,
            )
        return result

    def finish(source, inverse, here, value):
        scale = inverse[here, :]
        flat = source[here, :].astype(jnp.float32) * scale
        cosine = jnp.sum(flat * value, axis=1, keepdims=True)
        return (scale * (value - flat * cosine)).astype(jnp.bfloat16)

    def finish_images(c):
        def body(i, carry):
            here = pl.ds(pl.multiple_of(c * band + i * NORM_ROWS, NORM_ROWS), NORM_ROWS)
            value = direction[here, :] + image_returned[here, :].astype(jnp.float32)
            image_out[here, :] = finish(image_ref, image_inverse, here, value)
            return carry

        lax.fori_loop(0, band // NORM_ROWS, body, 0)

    def finish_text(c, start, part, buffer):
        def body(i, carry):
            at = pl.multiple_of(c * chunk + i * NORM_ROWS, NORM_ROWS)
            local = pl.ds(at, NORM_ROWS)
            here = pl.ds(pl.multiple_of(start + at, NORM_ROWS), NORM_ROWS)
            value = partial[part, local, :] + returned[buffer, local, :].astype(jnp.float32)
            text_out[here, :] = finish(text_ref, text_inverse, here, value)
            return carry

        lax.fori_loop(0, chunk // NORM_ROWS, body, 0)

    def unit_f(c):
        if c == 0:
            loads[0].wait()
        normalize(text_ref, text_inverse, captions.at[F0], start_f, c * chunk, chunk)

    def unit_n(c):
        if c == 0:
            loads[1].wait()
        normalize(text_ref, text_inverse, captions.at[N0], start_n, c * chunk, chunk)

    def unit_image(c):
        if c == 0:
            loads[2].wait()
            loads[3].wait()
        normalize(image_ref, image_inverse, image_unit, 0, c * band, band)

    def put_far(low):
        def run(c):
            @pl.when((until == 0) & (even if low else odd))
            def _():
                send(FAR, IN_F2, captions.at[F0], far_two, c)

            if not low:
                @pl.when(until > 0)
                def _():
                    send(FAR, IN_F1, captions.at[F0], far, c)

        return run

    def put_split(low):
        def run(c):
            @pl.when((until == 1) & (even if low else odd))
            def _():
                send(SPLIT, IN_F2, captions.at[F0], far_two, c)

        return run

    def put_near(low):
        wraps = (since == 0) & odd

        def run(c):
            @pl.when(wraps if low else jnp.logical_not(wraps))
            def _():
                send(NEAR, IN_N1, captions.at[N0], near, c)

        return run

    def put_image(c):
        send(IMAGE, IN_IMAGE, image_unit, pair, c)

    def hop(condition, op):
        def run(c):
            @pl.when(condition)
            def _():
                if starts((op, c), (TILE_F1, c)):
                    receive(IN_F1, c)
                send(HOP, IN_F2, captions.at[F1], far, c)

        return run

    def turn_back(c):
        @pl.when(since == 1)
        def _():
            if starts((TURN_BACK, c), (CROSS_F2, c)):
                receive(IN_F2, c)
            send(TURN, IN_F1, captions.at[F2], near, c)

    def tile_f0(c):
        keep(F0, None, tile(F0, image_unit, OWN_F0, None, start_f))

    def tile_n0(c):
        keep(N0, None, tile(N0, image_unit, OWN_N0, None, start_n))

    def tile_f1(c):
        waits = (since == 0) | (until == 0)
        if not starts((HOP_FIRST, c), (TILE_F1, c)):
            waits = waits | first
        if not starts((HOP_LATER, c), (TILE_F1, c)):
            waits = waits | later

        @pl.when(waits)
        def _():
            receive(IN_F1, c)

        keep(F1, c, tile(F1, image_unit, OWN_F1, c))

    def tile_n1(c):
        receive(IN_N1, c)
        keep(N1, c, tile(N1, image_unit, OWN_N1, c))

    def cross(slot, table, c, whole=False):
        if (CROSSES[0], 0) == (slot, c):
            for i in range(CHUNKS):
                receive(IN_IMAGE, i)
        return tile(slot, pair_unit, table, None if whole else c)

    def cross_n0(c):
        add(N0, None, cross(N0, PAIR_N0, c, True))

    def cross_n1(c):
        give(2, c, partial[N1, piece(c), :] + cross(N1, PAIR_N1, c))
        send(SUM_N1, HOME_N, staged.at[2], far, c)

    def cross_f1(c):
        add(F1, c, cross(F1, PAIR_F1, c))

        @pl.when(since == 0)
        def _():
            give(1, c, partial[F1, piece(c), :])
            send(SUM_F1, BACK_F1, staged.at[1], far, c)

        @pl.when(until == 0)
        def _():
            give(1, c, partial[F1, piece(c), :])
            send(SUM_F1, HOME, staged.at[1], near, c)

    def cross_f2(c):
        waits = since != 1
        if not starts((TURN_BACK, c), (CROSS_F2, c)):
            waits = since >= 0

        @pl.when(waits)
        def _():
            receive(IN_F2, c)

        keep(F2, c, cross(F2, PAIR_F2, c))

        @pl.when(since == 0)
        def _():
            give(0, c, partial[F2, piece(c), :])
            send(SUM_F2, HOME_SPLIT, staged.at[0], near_two, c)

        @pl.when(since > 1)
        def _():
            give(0, c, partial[F2, piece(c), :])
            send(SUM_F2, BACK_F2, staged.at[0], near, c)

    def pass_f2(c):
        @pl.when(since == 1)
        def _():
            receive(BACK_F1, c)
            arrived = returned[1, piece(c), :].astype(jnp.float32)
            give(0, c, arrived + partial[F2, piece(c), :])
            send(SUM_F2, HOME, staged.at[0], near_two, c)

    def pass_f1(condition):
        def run(c):
            @pl.when(condition)
            def _():
                receive(BACK_F2, c)
                arrived = returned[0, piece(c), :].astype(jnp.float32)
                give(1, c, arrived + partial[F1, piece(c), :])
                send(SUM_F1, HOME, staged.at[1], near, c)

        return run

    pair_terms = ((PAIR_F1, F1), (PAIR_F2, F2), (PAIR_N0, N0), (PAIR_N1, N1))
    own_terms = ((OWN_F0, F0), (OWN_F1, F1), (OWN_N0, N0), (OWN_N1, N1))

    def gather_pair(c):
        image_staged[stripe(c), :] = gather(c, pair_terms).astype(jnp.bfloat16)
        send(SUM_IMAGE, HOME_IMAGE, image_staged, pair, c)

    def gather_own(c):
        direction[stripe(c), :] = gather(c, own_terms)

    def end_image(c):
        receive(HOME_IMAGE, c)
        finish_images(c)

    def end_n(c):
        receive(HOME_N, c)
        finish_text(c, start_n, N0, 4)

    def end_f(c):
        receive(HOME, c)

        @pl.when(until == 1)
        def _():
            receive(HOME_SPLIT, c)
            add(F0, c, returned[3, piece(c), :].astype(jnp.float32))

        finish_text(c, start_f, F0, 2)

    steps = {
        UNIT_F: unit_f,
        UNIT_N: unit_n,
        UNIT_IMAGE: unit_image,
        ENTER: lambda c: enter(),
        READY: lambda c: ready(),
        PUT_FAR: put_far(False),
        PUT_FAR_LOW: put_far(True),
        PUT_NEAR: put_near(False),
        PUT_NEAR_LOW: put_near(True),
        PUT_SPLIT: put_split(False),
        PUT_SPLIT_LOW: put_split(True),
        PUT_IMAGE: put_image,
        HOP_FIRST: hop(first, HOP_FIRST),
        HOP_LATER: hop(later, HOP_LATER),
        TURN_BACK: turn_back,
        TILE_F0: tile_f0,
        TILE_N0: tile_n0,
        TILE_F1: tile_f1,
        TILE_N1: tile_n1,
        CROSS_N0: cross_n0,
        CROSS_N1: cross_n1,
        CROSS_F1: cross_f1,
        CROSS_F2: cross_f2,
        PASS_F2: pass_f2,
        PASS_F1_FIRST: pass_f1(first),
        PASS_F1_LATER: pass_f1(later),
        GATHER_PAIR: gather_pair,
        GATHER_OWN: gather_own,
        END_IMAGE: end_image,
        END_N: end_n,
        END_F: end_f,
    }
    for name, c in ORDER:
        steps[name](c)

    sent(FAR, captions.at[F0], piece)
    sent(NEAR, captions.at[N0], piece)
    sent(IMAGE, image_unit, stripe)
    sent(SUM_F2, staged.at[0], piece)
    sent(SUM_F1, staged.at[1], piece)
    sent(SUM_N1, staged.at[2], piece)
    sent(SUM_IMAGE, image_staged, stripe)

    @pl.when(until == 1)
    def _():
        sent(SPLIT, captions.at[F0], piece)

    @pl.when((since > 0) & (until > 0))
    def _():
        sent(HOP, captions.at[F1], piece)

    @pl.when(since == 1)
    def _():
        sent(TURN, captions.at[F2], piece)


def store(image_grad, text_grad, image_out, text_out, sem):
    parts = sem.shape[1]
    share = image_grad.shape[0] // parts
    copies = [
        pltpu.make_async_copy(
            source.at[pl.ds(c * share, share)], target.at[pl.ds(c * share, share)], sem.at[n, c]
        )
        for c in range(parts)
        for n, (source, target) in enumerate(((image_grad, image_out), (text_grad, text_out)))
    ]
    for copy in copies:
        copy.start()
    for copy in copies:
        copy.wait()


def solution(mesh):
    groups = mesh.shape["grp"]
    total = mesh.shape["blk"] * groups

    def local(images, texts, positions, exponent, offset):
        rows, width = images.shape
        half = rows // 2
        vmem = pl.BlockSpec(memory_space=pltpu.VMEM)
        hbm = pl.BlockSpec(memory_space=pltpu.HBM)
        smem = pl.BlockSpec(memory_space=pltpu.SMEM)
        images, texts, positions = (
            pltpu.with_memory_space_constraint(x, pltpu.HBM) for x in (images, texts, positions)
        )
        grads = pl.pallas_call(
            functools.partial(kernel, groups, total),
            out_shape=(
                pltpu.VMEM((rows, width), jnp.bfloat16),
                pltpu.VMEM((rows, width), jnp.bfloat16),
            ),
            in_specs=[hbm, hbm, hbm, smem, smem],
            out_specs=(vmem, vmem),
            scratch_shapes=[
                pltpu.VMEM((rows, width), jnp.bfloat16),
                pltpu.VMEM((rows, width), jnp.bfloat16),
                pltpu.VMEM((1, rows), jnp.int32),
                pltpu.VMEM((rows, width), jnp.bfloat16),
                pltpu.VMEM((rows, width), jnp.bfloat16),
                pltpu.VMEM((5, half, width), jnp.bfloat16),
                pltpu.VMEM((8, half, rows), jnp.bfloat16),
                pltpu.VMEM((5, half, width), jnp.float32),
                pltpu.VMEM((3, half, width), jnp.bfloat16),
                pltpu.VMEM((5, half, width), jnp.bfloat16),
                pltpu.VMEM((rows, width), jnp.bfloat16),
                pltpu.VMEM((rows, width), jnp.bfloat16),
                pltpu.VMEM((rows, width), jnp.float32),
                pltpu.VMEM((rows, 1), jnp.float32),
                pltpu.VMEM((rows, 1), jnp.float32),
                pltpu.SemaphoreType.DMA((4,)),
                pltpu.SemaphoreType.DMA((10, CHUNKS)),
                pltpu.SemaphoreType.DMA((10, CHUNKS)),
                pltpu.SemaphoreType.REGULAR,
            ],
            compiler_params=pltpu.CompilerParams(
                collective_id=0, has_side_effects=True, vmem_limit_bytes=32 * 1024 * 1024
            ),
        )(images, texts, positions, exponent, offset)
        grads = tuple(pltpu.with_memory_space_constraint(g, pltpu.VMEM) for g in grads)
        return pl.pallas_call(
            store,
            out_shape=(jax.ShapeDtypeStruct((rows, width), jnp.bfloat16),) * 2,
            in_specs=[vmem, vmem],
            out_specs=(hbm, hbm),
            scratch_shapes=[pltpu.SemaphoreType.DMA((2, 4))],
        )(*grads)

    shard = P(("blk", "grp"), None)
    return jax.shard_map(
        local,
        mesh=mesh,
        in_specs=(shard, shard, shard, P(), P()),
        out_specs=(shard, shard),
        check_vma=False,
    )
```
